32 devices in a mesh: dp: 4 (over y, x), psg: 8 (over z, core).
Axes of the slice: x: 2, y: 2, z: 4, core: 2. Of those that a mesh axis runs over, the one named last changes fastest.
Arguments:
- queries: bfloat16 [4, 128, 2048], P('dp', None, 'psg'), may hold values from -4 to 4
- keys: bfloat16 [4, 16, 256, 2048], P('dp', 'psg'), may hold values from -4 to 4
- values: bfloat16 [4, 16, 256, 2048], P('dp', 'psg'), may hold values from -6 to 6
- lengths: int32 [4, 16], P('dp', 'psg'), may hold values from 16 to 256, as said below
- out_weight: bfloat16 [4096, 2048], P('psg'), may hold values from -0.125 to 0.125
- out_cotangent: bfloat16 [4, 128, 4096], P('dp', None, 'psg'), may hold values from -6 to 6
Outputs:
- layer_out: bfloat16 [4, 128, 4096], P('dp', None, 'psg')
- weight_grad: float32 [4096, 2048], P('psg')
- query_grad: bfloat16 [4, 128, 2048], P('dp', None, 'psg')
- key_grad: bfloat16 [4, 16, 256, 2048], P('dp', 'psg')
- value_grad: bfloat16 [4, 16, 256, 2048], P('dp', 'psg')
The draws below stay inside these ranges and needn't reach their ends.
Inputs may be any that keep to these rules, and one draw needn't show every extreme that they name: `lengths`: every passage has at least 16 valid tokens, counted from its start; in every question some passage has all 256.
All inputs are finite; a program needn't handle non-finite values.
Results may differ from the reference program's by a relative error of at most 0.025.
Values may be sent and summed in bfloat16 or wider, within the bound.
No kernel may reach another device: no remote copies, remote signals or barrier semaphores. Data moves between devices by JAX's collectives and lax.ppermute only.
A program may use at most 64 MiB of HBM per device.

```python
import jax
import jax.numpy as jnp
from jax import lax

MODEL_DIM = 4096
HEAD_COUNT = 32
HEAD_SIZE = 64
ANSWER_LEN = 128
PASSAGE_LEN = 256
INNER_DIM = 2048
QUESTIONS = 4
PASSAGES = 16


def paired_draw(key):
    base_key = jax.random.fold_in(key, 11)
    query_key, keys_key, scale_key = jax.random.split(base_key, 3)
    query_shape = (QUESTIONS, ANSWER_LEN, INNER_DIM)
    key_shape = (QUESTIONS, PASSAGES, PASSAGE_LEN, INNER_DIM)
    query_draw = 0.45 * jax.random.normal(query_key, query_shape, jnp.float32)
    key_draw = 0.45 * jax.random.normal(keys_key, key_shape, jnp.float32)
    scales = jnp.exp(jax.random.uniform(scale_key, (QUESTIONS, PASSAGES, PASSAGE_LEN, 1), jnp.float32, -0.5, 0.5))
    query_draw = jnp.clip(query_draw, -4.0, 4.0)
    key_draw = jnp.clip(key_draw * scales, -4.0, 4.0)
    return (query_draw, key_draw)


def draw_queries(key, part):
    return paired_draw(key)[0].astype(jnp.bfloat16)


def draw_keys(key, part):
    return paired_draw(key)[1].astype(jnp.bfloat16)


def draw_lengths(key, part):
    base_key = jax.random.fold_in(key, 23)
    first_key, second_key = jax.random.split(base_key, 2)
    drawn_lengths = jax.random.randint(first_key, (QUESTIONS, PASSAGES), 16, PASSAGE_LEN + 1)
    full_one = jax.random.randint(second_key, (QUESTIONS,), 0, PASSAGES)
    full_marks = jnp.arange(PASSAGES, dtype=jnp.int32)[None, :] == full_one[:, None]
    return jnp.where(full_marks, PASSAGE_LEN, drawn_lengths).astype(jnp.int32)


def level_of(stream_key, dims, cuts, low, top_value):
    def one(dim, blocks):
        draws = jax.random.uniform(jax.random.fold_in(jax.random.fold_in(stream_key, 6), dim), (blocks,), jnp.float32, low / len(cuts), top_value / len(cuts))
        return jnp.repeat(jnp.exp(draws), dims[dim] // blocks).reshape((-1,) + (1,) * (len(dims) - dim - 1))

    factor_of = one(*cuts[0])
    for cut in cuts[1:]:
        factor_of = factor_of * one(*cut)
    return factor_of


def gaussian(key, dims, scale, bound, shards=(), kind=jnp.bfloat16):
    drawn = jax.random.normal(key, dims, jnp.float32) * scale
    if len(shards) > 0:
        drawn = level_of(key, dims, shards, -0.22, 0.18) * drawn
    return jnp.clip(drawn, min=-bound, max=bound).astype(kind)


def setup_inputs(seed: int = 0) -> dict:
    key_of = jax.random.split(jax.random.key(seed), 7)
    queries = draw_queries(jax.random.fold_in(key_of[6], 71), 0)
    keys = draw_keys(jax.random.fold_in(key_of[6], 71), 0)
    values = gaussian(key_of[2], (QUESTIONS, PASSAGES, PASSAGE_LEN, INNER_DIM), 1.0, 6.0, ((0, 4), (1, 8)))
    lengths = draw_lengths(jax.random.fold_in(key_of[6], 71), 0)
    out_weight = gaussian(key_of[4], (MODEL_DIM, INNER_DIM), INNER_DIM ** -0.5, 0.125, ((0, 8),))
    out_cotangent = gaussian(key_of[5], (QUESTIONS, ANSWER_LEN, MODEL_DIM), 1.0, 6.0, ((0, 4), (2, 8)))
    return dict(queries=queries, keys=keys, values=values, lengths=lengths, out_weight=out_weight, out_cotangent=out_cotangent)


def head_slice(block, head_index):
    return lax.dynamic_slice_in_dim(block, head_index * HEAD_SIZE, HEAD_SIZE, 1)


def reference(queries, keys, values, lengths, out_weight, out_cotangent):
    question_count = queries.shape[0]
    key_count = PASSAGES * PASSAGE_LEN
    positions = jnp.arange(PASSAGE_LEN, dtype=jnp.int32)
    valid = (positions[None, None, :] < lengths[:, :, None]).reshape(question_count, key_count)
    keys_flat = keys.reshape(question_count, key_count, INNER_DIM)
    values_flat = values.reshape(question_count, key_count, INNER_DIM)
    head_ids = jnp.arange(HEAD_COUNT, dtype=jnp.int32)

    def forward_one(block):
        query_block, key_block, value_block, valid_block = block

        def one_head(head_index):
            query_head = head_slice(query_block, head_index)
            key_head = head_slice(key_block, head_index)
            value_head = head_slice(value_block, head_index)
            scores = jnp.dot(query_head, key_head.T, preferred_element_type=jnp.float32)
            row_max = jnp.max(jnp.where(valid_block[None, :], scores, -jnp.inf), axis=1)
            weights = jnp.where(valid_block[None, :], jnp.exp(scores - row_max[:, None]), 0.0)
            row_sum = jnp.sum(weights, axis=1)
            output = jnp.dot(weights.astype(jnp.bfloat16), value_head, preferred_element_type=jnp.float32) / row_sum[:, None]
            return output, row_max, row_sum

        output, row_max, row_sum = lax.map(one_head, head_ids)
        return jnp.transpose(output, (1, 0, 2)).reshape(ANSWER_LEN, INNER_DIM), row_max, row_sum

    output, row_max, row_sum = lax.map(forward_one, (queries, keys_flat, values_flat, valid))
    context = output.astype(jnp.bfloat16)
    context_rows = context.reshape(question_count * ANSWER_LEN, INNER_DIM)
    grad_rows = out_cotangent.reshape(question_count * ANSWER_LEN, MODEL_DIM)
    layer_out = jnp.dot(context_rows, out_weight.T, preferred_element_type=jnp.float32).astype(jnp.bfloat16)
    layer_out = layer_out.reshape(question_count, ANSWER_LEN, MODEL_DIM)
    weight_grad = jnp.dot(grad_rows.T, context_rows, preferred_element_type=jnp.float32)
    context_grad = jnp.dot(grad_rows, out_weight, preferred_element_type=jnp.float32).astype(jnp.bfloat16)
    context_grad = context_grad.reshape(question_count, ANSWER_LEN, INNER_DIM)
    products = context_grad.astype(jnp.float32) * context.astype(jnp.float32)
    row_dots = jnp.transpose(jnp.sum(products.reshape(question_count, ANSWER_LEN, HEAD_COUNT, HEAD_SIZE), axis=3), (0, 2, 1))

    def backward_one(block):
        query_block, key_block, value_block, valid_block, grad_block, max_block, sum_block, dots_block = block

        def one_head(head_index):
            query_head = head_slice(query_block, head_index)
            key_head = head_slice(key_block, head_index)
            value_head = head_slice(value_block, head_index)
            grad_head = head_slice(grad_block, head_index)
            scores = jnp.dot(query_head, key_head.T, preferred_element_type=jnp.float32)
            probs = jnp.where(valid_block[None, :], jnp.exp(scores - max_block[head_index][:, None]) / sum_block[head_index][:, None], 0.0)
            prob_grad = jnp.dot(grad_head, value_head.T, preferred_element_type=jnp.float32)
            score_grad = (probs * (prob_grad - dots_block[head_index][:, None])).astype(jnp.bfloat16)
            value_part = jnp.dot(probs.astype(jnp.bfloat16).T, grad_head, preferred_element_type=jnp.float32).astype(jnp.bfloat16)
            key_part = jnp.dot(score_grad.T, query_head, preferred_element_type=jnp.float32).astype(jnp.bfloat16)
            query_part = jnp.dot(score_grad, key_head, preferred_element_type=jnp.float32).astype(jnp.bfloat16)
            return query_part, key_part, value_part

        query_part, key_part, value_part = lax.map(one_head, head_ids)
        query_part = jnp.transpose(query_part, (1, 0, 2)).reshape(ANSWER_LEN, INNER_DIM)
        key_part = jnp.transpose(key_part, (1, 0, 2)).reshape(key_count, INNER_DIM)
        value_part = jnp.transpose(value_part, (1, 0, 2)).reshape(key_count, INNER_DIM)
        return query_part, key_part, value_part

    query_grad, key_grad, value_grad = lax.map(backward_one, (queries, keys_flat, values_flat, valid, context_grad, row_max, row_sum, row_dots))
    key_grad = key_grad.reshape(keys.shape)
    value_grad = value_grad.reshape(values.shape)
    return (layer_out, weight_grad, query_grad, key_grad, value_grad)
```

```python
import functools

import jax
import jax.numpy as jnp
from jax import lax
from jax.experimental import pallas as pl
from jax.experimental.pallas import tpu as pltpu
from jax.sharding import PartitionSpec as P

HEAD_SIZE = 64
PAIR = 2 * HEAD_SIZE
MASKED = -1e30

NT = (((1,), (1,)), ((), ()))
NN = (((1,), (0,)), ((), ()))
TN = (((0,), (0,)), ((), ()))
ANY = pl.BlockSpec(memory_space=pl.ANY)
VMEM = pl.BlockSpec(memory_space=pltpu.VMEM)
SMEM = pl.BlockSpec(memory_space=pltpu.SMEM)


def dot(a, b, dims):
    return lax.dot_general(a, b, dims, preferred_element_type=jnp.float32)


def swap(x, axis, size, distance):
    return lax.ppermute(x, axis, [(j, j ^ distance) for j in range(size)])


def gather_slots(x, axis, size):
    even = [x] + [None] * (size // 2 - 1)
    for d in range(size - 2, 0, -2):
        even[d // 2] = swap(x, axis, size, d)
    odd = [swap(e, axis, size, 1) for e in even]
    return even, odd


def block_stack(x, lane_low):
    zero = jnp.zeros_like(x)
    return jnp.concatenate([jnp.where(lane_low, x, zero), jnp.where(lane_low, zero, x)], axis=0)


def diagonal(x):
    rows = x.shape[1] // 2
    return jnp.concatenate([x[:HEAD_SIZE, :rows], x[HEAD_SIZE:, rows:]], axis=0)


def valid_rows(lengths_ref, passages, passage_len):
    row = lax.broadcasted_iota(jnp.int32, (passage_len, 1), 0)
    return jnp.concatenate([row < lengths_ref[0, p] for p in range(passages)], axis=0)


def columns_of(ref, me, slot, width):
    owner = jnp.bitwise_xor(me, slot)
    return ref.at[:, pl.ds(pl.multiple_of(owner * width, width), width)]


def forward_kernel(size, passages, me_ref, lengths_ref, *refs):
    q_refs = refs[:size]
    keys_ref, values_ref, even_ref, odd_ref, even_lse, odd_lse, q_buf, k_buf, v_buf, sem = refs[size:]
    me = me_ref[0]
    width = q_buf.shape[2]
    half = size // 2

    def k_copy(s):
        return pltpu.make_async_copy(columns_of(keys_ref, me, s, width), k_buf.at[s], sem.at[0, s])

    def v_copy(s):
        return pltpu.make_async_copy(columns_of(values_ref, me, s, width), v_buf.at[s], sem.at[1, s])

    for s in range(size):
        k_copy(s).start()
        v_copy(s).start()
    for s in range(size):
        q_buf[s] = q_refs[s][...]
    key_count = k_buf.shape[1]
    valid = valid_rows(lengths_ref, passages, key_count // passages)
    lane_low = lax.broadcasted_iota(jnp.int32, (1, PAIR), 1) < HEAD_SIZE

    def one_slot(s, out_ref, lse_ref, k):
        k_copy(s).wait()
        v_copy(s).wait()
        rows = []
        for p in range(width // PAIR):
            lanes = slice(p * PAIR, (p + 1) * PAIR)
            queries = block_stack(q_buf[s, :, lanes], lane_low)
            scores = jnp.where(valid, dot(k_buf[s, :, lanes], queries, NT), MASKED)
            top = jnp.max(scores, axis=0, keepdims=True)
            weights = jnp.exp(scores - top)
            total = jnp.sum(weights, axis=0, keepdims=True)
            mixed = dot(v_buf[s, :, lanes], weights.astype(jnp.bfloat16), TN) / total
            out_ref[k, lanes, :] = diagonal(mixed).astype(jnp.bfloat16)
            lse = top + jnp.log(total)
            n = lse.shape[1] // 2
            rows += [lse[:, :n], lse[:, n:]]
        lse_ref[k] = jnp.concatenate(rows, axis=0)

    def body(k, carry):
        one_slot(2 * k, even_ref, even_lse, k)
        one_slot(2 * k + 1, odd_ref, odd_lse, k)
        return carry

    lax.fori_loop(0, half, body, 0)


def merge(parts, lses):
    top = functools.reduce(jnp.maximum, lses)
    total = sum(jnp.exp(x - top) for x in lses)
    lse = top + jnp.log(total)
    outs = []
    for h in range(lse.shape[0]):
        rows = slice(h * HEAD_SIZE, (h + 1) * HEAD_SIZE)
        outs.append(
            sum(jnp.exp(x[h : h + 1] - lse[h : h + 1]) * p[rows].astype(jnp.float32) for p, x in zip(parts, lses))
        )
    return jnp.concatenate(outs, axis=0), lse


def merge_pair_kernel(a_ref, a_lse, b_ref, b_lse, out_ref, lse_ref):
    for k in range(a_ref.shape[0]):
        out, lse = merge([a_ref[k], b_ref[k]], [a_lse[k], b_lse[k]])
        out_ref[k] = out.astype(jnp.bfloat16)
        lse_ref[k] = lse


def merge_final_kernel(count, *refs):
    first_ref, first_lse = refs[:2]
    others = refs[2 : 2 + 2 * (count - 1)]
    grad_ref, context_ref, stats_ref = refs[2 + 2 * (count - 1) :]
    parts = [first_ref[0]] + [r[...] for r in others[0::2]]
    lses = [first_lse[0]] + [r[...] for r in others[1::2]]
    out, lse = merge(parts, lses)
    context = out.T.astype(jnp.bfloat16)
    context_ref[...] = context
    product = (context.astype(jnp.float32) * grad_ref[...].astype(jnp.float32)).T
    dots = [
        jnp.sum(product[h * HEAD_SIZE : (h + 1) * HEAD_SIZE], axis=0, keepdims=True) for h in range(lse.shape[0])
    ]
    stats_ref[...] = jnp.concatenate([lse] + dots, axis=0)


def backward_kernel(size, passages, me_ref, lengths_ref, *refs):
    q_refs, g_refs, stats_refs = refs[:size], refs[size : 2 * size], refs[2 * size : 3 * size]
    (keys_ref, values_ref, dk_ref, dv_ref, even_ref, odd_ref, q_buf, g_buf, st_buf, k_buf, v_buf, dk_buf, dv_buf, sem) = (
        refs[3 * size :]
    )
    me = me_ref[0]
    width = q_buf.shape[2]
    half = size // 2

    def k_copy(s):
        return pltpu.make_async_copy(columns_of(keys_ref, me, s, width), k_buf.at[s], sem.at[0, s])

    def v_copy(s):
        return pltpu.make_async_copy(columns_of(values_ref, me, s, width), v_buf.at[s], sem.at[1, s])

    def dk_copy(s):
        return pltpu.make_async_copy(dk_buf.at[s], columns_of(dk_ref, me, s, width), sem.at[2, s])

    def dv_copy(s):
        return pltpu.make_async_copy(dv_buf.at[s], columns_of(dv_ref, me, s, width), sem.at[3, s])

    for s in range(size):
        k_copy(s).start()
        v_copy(s).start()
    for s in range(size):
        q_buf[s] = q_refs[s][...]
        g_buf[s] = g_refs[s][...]
        st_buf[s] = stats_refs[s][...]
    key_count = k_buf.shape[1]
    valid = valid_rows(lengths_ref, passages, key_count // passages)
    lane_low = lax.broadcasted_iota(jnp.int32, (1, PAIR), 1) < HEAD_SIZE
    heads = width // HEAD_SIZE

    def one_slot(s, out_ref, k):
        k_copy(s).wait()
        v_copy(s).wait()
        for p in range(width // PAIR):
            lanes = slice(p * PAIR, (p + 1) * PAIR)
            queries = block_stack(q_buf[s, :, lanes], lane_low)
            grads = block_stack(g_buf[s, :, lanes], lane_low)
            stats = st_buf[s]
            lse = jnp.concatenate([stats[2 * p : 2 * p + 1], stats[2 * p + 1 : 2 * p + 2]], axis=1)
            dots = jnp.concatenate(
                [stats[heads + 2 * p : heads + 2 * p + 1], stats[heads + 2 * p + 1 : heads + 2 * p + 2]], axis=1
            )
            key_block = k_buf[s, :, lanes]
            scores = jnp.where(valid, dot(key_block, queries, NT), MASKED)
            probs = jnp.exp(scores - lse)
            prob_grad = dot(v_buf[s, :, lanes], grads, NT)
            score_grad = (probs * (prob_grad - dots)).astype(jnp.bfloat16)
            dv_buf[s, :, lanes] = dot(probs.astype(jnp.bfloat16), grads, NN).astype(jnp.bfloat16)
            dk_buf[s, :, lanes] = dot(score_grad, queries, NN).astype(jnp.bfloat16)
            out_ref[k, lanes, :] = diagonal(dot(key_block, score_grad, TN)).astype(jnp.bfloat16)
        dk_copy(s).start()
        dv_copy(s).start()

    def body(k, carry):
        one_slot(2 * k, even_ref, k)
        one_slot(2 * k + 1, odd_ref, k)
        return carry

    lax.fori_loop(0, half, body, 0)
    for s in range(size):
        dk_copy(s).wait()
        dv_copy(s).wait()


def sum_transposed_kernel(first_ref, *refs):
    out_ref = refs[-1]
    total = first_ref[0].astype(jnp.float32)
    for r in refs[:-1]:
        total += r[...].astype(jnp.float32)
    out_ref[...] = total.T.astype(jnp.bfloat16)


def grad_partial_kernel(size, me_ref, cot_ref, weight_ref, even_ref, odd_ref, w_buf, sem):
    me = me_ref[0]
    width = w_buf.shape[2]

    def w_copy(s):
        return pltpu.make_async_copy(columns_of(weight_ref, me, s, width), w_buf.at[s], sem.at[s])

    order = list(range(1, size, 2)) + list(range(0, size, 2))
    for s in order:
        w_copy(s).start()
    cot = cot_ref[...]
    for s in order:
        w_copy(s).wait()
        (odd_ref if s % 2 else even_ref)[s // 2] = dot(cot, w_buf[s], NN).astype(jnp.bfloat16)


def layer_out_kernel(size, me_ref, even_ref, odd_ref, weight_ref, out_ref, w_buf, sem):
    me = me_ref[0]
    width = w_buf.shape[2]

    def w_copy(s):
        return pltpu.make_async_copy(columns_of(weight_ref, me, s, width), w_buf.at[s], sem.at[s])

    for s in range(size):
        w_copy(s).start()
    total = None
    for s in range(size):
        w_copy(s).wait()
        part = dot((odd_ref if s % 2 else even_ref)[s // 2], w_buf[s], NT)
        total = part if total is None else total + part
    out_ref[...] = total.astype(jnp.bfloat16)


def weight_grad_kernel(size, groups, me_ref, *refs):
    cots = refs[:groups]
    evens, odds = refs[groups : 2 * groups], refs[2 * groups : 3 * groups]
    out_ref, cot_buf, out_buf, sem = refs[3 * groups :]
    me = me_ref[0]
    width = out_buf.shape[2]
    rows = cots[0].shape[0]
    for g in range(groups):
        cot_buf[:, g * rows : (g + 1) * rows] = cots[g][...].T

    def out_copy(s):
        return pltpu.make_async_copy(out_buf.at[s], columns_of(out_ref, me, s, width), sem.at[s])

    for s in range(size):
        context = jnp.concatenate([(odds if s % 2 else evens)[g][s // 2] for g in range(groups)], axis=0)
        out_buf[s] = dot(cot_buf[...], context, NN)
        out_copy(s).start()
    for s in range(size):
        out_copy(s).wait()


def shaped(shape, dtype):
    return jax.ShapeDtypeStruct(shape, dtype)


def fast_device(dp, size, queries, keys, values, lengths, out_weight, out_cotangent):
    bf16, f32 = jnp.bfloat16, jnp.float32
    passages, passage_len, inner = keys.shape[1:]
    key_count = passages * passage_len
    answers, width = queries.shape[1:]
    half = size // 2
    heads = width // HEAD_SIZE
    model = out_weight.shape[0]
    me = lax.axis_index("psg").reshape(1)
    query = queries[0]
    cot = out_cotangent[0]
    key_rows = keys.reshape(key_count, inner)
    value_rows = values.reshape(key_count, inner)

    q_even, q_odd = gather_slots(query, "psg", size)
    cots = [cot] + [swap(cot, "dp", dp, d) for d in range(1, dp)]

    g_even, g_odd = pl.pallas_call(
        functools.partial(grad_partial_kernel, size),
        out_shape=[shaped((half, answers, width), bf16)] * 2,
        in_specs=[SMEM, VMEM, ANY],
        out_specs=[VMEM, VMEM],
        scratch_shapes=[pltpu.VMEM((size, model, width), bf16), pltpu.SemaphoreType.DMA((size,))],
        name="grad_partial",
    )(me, cot, out_weight)
    g_other = swap(g_odd, "psg", size, 1)
    g_sum = (g_even.astype(f32) + g_other.astype(f32)).astype(bf16)
    g_parts = [swap(g_sum[d // 2], "psg", size, d) for d in range(size - 2, 0, -2)]
    context_grad = g_sum[0].astype(f32)
    for part in g_parts:
        context_grad = context_grad + part.astype(f32)
    context_grad = context_grad.astype(bf16)

    slots = [r for pair in zip(q_even, q_odd) for r in pair]
    o_even, o_odd, l_even, l_odd = pl.pallas_call(
        functools.partial(forward_kernel, size, passages),
        out_shape=[shaped((half, width, answers), bf16)] * 2 + [shaped((half, heads, answers), f32)] * 2,
        in_specs=[SMEM, SMEM] + [VMEM] * size + [ANY, ANY],
        out_specs=[VMEM] * 4,
        scratch_shapes=[
            pltpu.VMEM((size, answers, width), bf16),
            pltpu.VMEM((size, key_count, width), bf16),
            pltpu.VMEM((size, key_count, width), bf16),
            pltpu.SemaphoreType.DMA((2, size)),
        ],
        name="attention_forward",
    )(me, lengths, *slots, key_rows, value_rows)

    o_other, l_other = swap(o_odd, "psg", size, 1), swap(l_odd, "psg", size, 1)
    o_pair, l_pair = pl.pallas_call(
        merge_pair_kernel,
        out_shape=[shaped((half, width, answers), bf16), shaped((half, heads, answers), f32)],
        in_specs=[VMEM] * 4,
        out_specs=[VMEM] * 2,
        name="merge_pair",
    )(o_even, l_even, o_other, l_other)
    arrived = []
    for d in range(size - 2, 0, -2):
        arrived += [swap(o_pair[d // 2], "psg", size, d), swap(l_pair[d // 2], "psg", size, d)]
    context, stats = pl.pallas_call(
        functools.partial(merge_final_kernel, half),
        out_shape=[shaped((answers, width), bf16), shaped((2 * heads, answers), f32)],
        in_specs=[VMEM] * (2 * half + 1),
        out_specs=[VMEM] * 2,
        name="merge_final",
    )(o_pair, l_pair, *arrived, context_grad)

    s_even, s_odd = gather_slots(stats, "psg", size)
    cg_even, cg_odd = gather_slots(context_grad, "psg", size)
    g_slots = [r for pair in zip(cg_even, cg_odd) for r in pair]
    s_slots = [r for pair in zip(s_even, s_odd) for r in pair]
    key_grad, value_grad, dq_even, dq_odd = pl.pallas_call(
        functools.partial(backward_kernel, size, passages),
        out_shape=[shaped((key_count, inner), bf16)] * 2 + [shaped((half, width, answers), bf16)] * 2,
        in_specs=[SMEM, SMEM] + [VMEM] * (3 * size) + [ANY, ANY],
        out_specs=[ANY, ANY, VMEM, VMEM],
        scratch_shapes=[
            pltpu.VMEM((size, answers, width), bf16),
            pltpu.VMEM((size, answers, width), bf16),
            pltpu.VMEM((size, 2 * heads, answers), f32),
        ]
        + [pltpu.VMEM((size, key_count, width), bf16)] * 4
        + [pltpu.SemaphoreType.DMA((4, size))],
        name="attention_backward",
    )(me, lengths, *slots, *g_slots, *s_slots, key_rows, value_rows)

    c_even = [context] + [None] * (half - 1)
    for d in range(size - 2, 0, -2):
        c_even[d // 2] = swap(context, "psg", size, d)
    own_even = jnp.stack(c_even)
    evens = [own_even] + [swap(own_even, "dp", dp, d) for d in range(1, dp)]
    odds = [swap(e, "psg", size, 1) for e in evens]
    layer_out = pl.pallas_call(
        functools.partial(layer_out_kernel, size),
        out_shape=shaped((answers, model), bf16),
        in_specs=[SMEM, VMEM, VMEM, ANY],
        out_specs=VMEM,
        scratch_shapes=[pltpu.VMEM((size, model, width), bf16), pltpu.SemaphoreType.DMA((size,))],
        name="layer_out",
    )(me, evens[0], odds[0], out_weight)
    weight_grad = pl.pallas_call(
        functools.partial(weight_grad_kernel, size, dp),
        out_shape=shaped((model, inner), f32),
        in_specs=[SMEM] + [VMEM] * (3 * dp),
        out_specs=ANY,
        scratch_shapes=[
            pltpu.VMEM((model, dp * answers), bf16),
            pltpu.VMEM((size, model, width), f32),
            pltpu.SemaphoreType.DMA((size,)),
        ],
        name="weight_grad",
    )(me, *cots, *evens, *odds)

    dq_other = swap(dq_odd, "psg", size, 1)
    dq_sum = (dq_even.astype(f32) + dq_other.astype(f32)).astype(bf16)
    dq_parts = [swap(dq_sum[d // 2], "psg", size, d) for d in range(size - 2, 0, -2)]
    query_grad = pl.pallas_call(
        sum_transposed_kernel,
        out_shape=shaped((answers, width), bf16),
        in_specs=[VMEM] * half,
        out_specs=VMEM,
        name="query_sum",
    )(dq_sum, *dq_parts)
    return (
        layer_out[None],
        weight_grad,
        query_grad[None],
        key_grad.reshape(keys.shape),
        value_grad.reshape(values.shape),
    )


def spread_heads(factor):
    return jnp.transpose(factor, (0, 2, 1))[..., None]


def general_device(queries, keys, values, lengths, out_weight, out_cotangent):
    question_count, passages, passage_len, inner_dim = keys.shape
    key_count = passages * passage_len
    answer_len = queries.shape[1]
    head_split = (question_count, answer_len, inner_dim // HEAD_SIZE, HEAD_SIZE)
    key_split = (question_count, key_count, inner_dim // HEAD_SIZE, HEAD_SIZE)
    einsum = functools.partial(jnp.einsum, preferred_element_type=jnp.float32)
    query_heads = lax.all_gather(queries, "psg", axis=2, tiled=True).reshape(head_split)
    key_heads = keys.reshape(key_split)
    value_heads = values.reshape(key_split)
    positions = jnp.arange(passage_len, dtype=jnp.int32)
    valid = (positions[None, None, :] < lengths[:, :, None]).reshape(question_count, 1, 1, key_count)
    scores = einsum("bihe,bkhe->bhik", query_heads, key_heads)
    row_max = lax.pmax(jnp.max(jnp.where(valid, scores, -jnp.inf), axis=3), "psg")
    weights = jnp.where(valid, jnp.exp(scores - row_max[..., None]), 0.0)
    output = einsum("bhik,bkhe->bihe", weights.astype(jnp.bfloat16), value_heads)
    row_sum, output = lax.psum((jnp.sum(weights, axis=3), output), "psg")
    context = (output / spread_heads(row_sum)).astype(jnp.bfloat16)
    context_rows = context.reshape(question_count * answer_len, inner_dim)
    grad_rows = out_cotangent.reshape(question_count * answer_len, -1)
    layer_out = jnp.dot(context_rows, out_weight.T, preferred_element_type=jnp.float32).astype(jnp.bfloat16)
    weight_grad = lax.psum(
        jnp.dot(grad_rows.T, context_rows, preferred_element_type=jnp.float32).astype(jnp.bfloat16), "dp"
    ).astype(jnp.float32)
    context_grad = lax.psum(jnp.dot(grad_rows, out_weight, preferred_element_type=jnp.float32), "psg").astype(
        jnp.bfloat16
    )
    grad_heads = context_grad.reshape(head_split)
    products = grad_heads.astype(jnp.float32) * context.astype(jnp.float32)
    row_dots = jnp.transpose(jnp.sum(products, axis=3), (0, 2, 1))
    probs = weights / row_sum[..., None]
    prob_grad = einsum("bihe,bkhe->bhik", grad_heads, value_heads)
    score_grad = (probs * (prob_grad - row_dots[..., None])).astype(jnp.bfloat16)
    value_grad = einsum("bhik,bihe->bkhe", probs.astype(jnp.bfloat16), grad_heads)
    key_grad = einsum("bhik,bihe->bkhe", score_grad, query_heads)
    query_terms = einsum("bhik,bkhe->bihe", score_grad, key_heads).reshape(question_count, answer_len, inner_dim)
    query_grad = lax.psum_scatter(query_terms, "psg", scatter_dimension=2, tiled=True)
    return (
        layer_out.reshape(question_count, answer_len, -1),
        weight_grad,
        query_grad.astype(jnp.bfloat16),
        key_grad.astype(jnp.bfloat16).reshape(keys.shape),
        value_grad.astype(jnp.bfloat16).reshape(values.shape),
    )


def per_device(dp, size, queries, keys, values, lengths, out_weight, out_cotangent):
    width = queries.shape[2]
    direct = (
        size in (2, 4, 8)
        and dp in (1, 2, 4)
        and keys.shape[0] == 1
        and width % PAIR == 0
        and queries.shape[1] % 128 == 0
        and keys.shape[2] % 16 == 0
        and out_weight.shape[0] % 128 == 0
    )
    arguments = (queries, keys, values, lengths, out_weight, out_cotangent)
    return fast_device(dp, size, *arguments) if direct else general_device(*arguments)


def solution(mesh):
    return jax.shard_map(
        functools.partial(per_device, mesh.shape["dp"], mesh.shape["psg"]),
        mesh=mesh,
        in_specs=(
            P("dp", None, "psg"),
            P("dp", "psg", None, None),
            P("dp", "psg", None, None),
            P("dp", "psg"),
            P("psg", None),
            P("dp", None, "psg"),
        ),
        out_specs=(
            P("dp", None, "psg"),
            P("psg", None),
            P("dp", None, "psg"),
            P("dp", "psg", None, None),
            P("dp", "psg", None, None),
        ),
        check_vma=False,
    )
```

```python
import functools

import jax
import jax.numpy as jnp
from jax import lax
from jax.experimental import pallas as pl
from jax.experimental.pallas import tpu as pltpu
from jax.sharding import PartitionSpec as P

HEAD_SIZE = 64
PAIR = 2 * HEAD_SIZE
MASKED = -1e30
EXTRA = 16
MIB = 1 << 20

NT = (((1,), (1,)), ((), ()))
NN = (((1,), (0,)), ((), ()))
TN = (((0,), (0,)), ((), ()))
ANY = pl.BlockSpec(memory_space=pl.ANY)
VMEM = pl.BlockSpec(memory_space=pltpu.VMEM)
SMEM = pl.BlockSpec(memory_space=pltpu.SMEM)


def dot(a, b, dims):
    return lax.dot_general(a, b, dims, preferred_element_type=jnp.float32)


def swap(x, axis, size, distance):
    return lax.ppermute(x, axis, [(j, j ^ distance) for j in range(size)])


def call(kernel, *args, out, ins, outs, scratch=(), vmem=8, alias=None):
    return pl.pallas_call(
        kernel,
        out_shape=out,
        in_specs=ins,
        out_specs=outs,
        scratch_shapes=list(scratch),
        input_output_aliases=alias or {},
        compiler_params=pltpu.CompilerParams(vmem_limit_bytes=vmem * MIB),
    )(*args)


def far_first(size):
    return range(size - 2, 0, -2)


def spread(x, size):
    even = [x] + [None] * (size // 2 - 1)
    for d in far_first(size):
        even[d // 2] = swap(x, "psg", size, d)
    return even


def across(blocks, size):
    return [swap(b, "psg", size, 1) for b in blocks]


def block_stack(x, lane_low):
    zero = jnp.zeros_like(x)
    return jnp.concatenate([jnp.where(lane_low, x, zero), jnp.where(lane_low, zero, x)], axis=0)


def diagonal(x):
    rows = x.shape[1] // 2
    return jnp.concatenate([x[:HEAD_SIZE, :rows], x[HEAD_SIZE:, rows:]], axis=0)


def mask_bias(lengths_ref, passages, passage_len):
    row = lax.broadcasted_iota(jnp.int32, (passage_len, PAIR), 0)
    return jnp.concatenate([jnp.where(row < lengths_ref[0, p], 0.0, MASKED) for p in range(passages)], axis=0)


def thirds(x):
    high = x.astype(jnp.bfloat16)
    rest = x - high.astype(jnp.float32)
    middle = rest.astype(jnp.bfloat16)
    low = (rest - middle.astype(jnp.float32)).astype(jnp.bfloat16)
    parts = [high.astype(jnp.float32), middle.astype(jnp.float32), low.astype(jnp.float32)]
    pad = EXTRA - 3 * x.shape[0]
    return jnp.concatenate(parts + [jnp.zeros((pad, x.shape[1]), jnp.float32)], axis=0).astype(jnp.bfloat16)


def unite(rows, heads):
    wide = rows.astype(jnp.float32)
    return wide[:heads] + wide[heads : 2 * heads] + wide[2 * heads : 3 * heads]


def columns_of(ref, me, slot, width):
    owner = jnp.bitwise_xor(me, slot)
    return ref.at[:, pl.ds(pl.multiple_of(owner * width, width), width)]


def forward_kernel(size, passages, me_ref, lengths_ref, *refs):
    q_refs = refs[:size]
    keys_ref, values_ref, even_ref, odd_ref, q_buf, k_buf, v_buf, bias_ref, sem = refs[size:]
    me = me_ref[0]
    width = q_buf.shape[2]
    half = size // 2

    def k_copy(s):
        return pltpu.make_async_copy(columns_of(keys_ref, me, s, width), k_buf.at[s], sem.at[0, s])

    def v_copy(s):
        return pltpu.make_async_copy(columns_of(values_ref, me, s, width), v_buf.at[s], sem.at[1, s])

    for s in range(size):
        k_copy(s).start()
        v_copy(s).start()
    for s in range(size):
        q_buf[s] = q_refs[s][...]
    bias_ref[...] = mask_bias(lengths_ref, passages, k_buf.shape[1] // passages)
    lane_low = lax.broadcasted_iota(jnp.int32, (1, PAIR), 1) < HEAD_SIZE

    def one_slot(s, out_ref, k):
        k_copy(s).wait()
        v_copy(s).wait()
        rows = []
        for p in range(width // PAIR):
            lanes = slice(p * PAIR, (p + 1) * PAIR)
            queries = block_stack(q_buf[s, :, lanes], lane_low)
            bias = bias_ref[...]
            scores = dot(k_buf[s, :, lanes], queries, NT) + jnp.concatenate([bias, bias], axis=1)
            top = jnp.max(scores, axis=0, keepdims=True)
            weights = jnp.exp(scores - top)
            total = jnp.sum(weights, axis=0, keepdims=True)
            mixed = dot(v_buf[s, :, lanes], weights.astype(jnp.bfloat16), TN) / total
            out_ref[k, lanes, :] = diagonal(mixed).astype(jnp.bfloat16)
            lse = top + jnp.log(total)
            n = lse.shape[1] // 2
            rows += [lse[:, :n], lse[:, n:]]
        out_ref[k, width:, :] = thirds(jnp.concatenate(rows, axis=0))

    def body(k, carry):
        one_slot(2 * k, even_ref, k)
        one_slot(2 * k + 1, odd_ref, k)
        return carry

    lax.fori_loop(0, half, body, 0)


def merge(blocks):
    width = blocks[0].shape[0] - EXTRA
    heads = width // HEAD_SIZE
    lses = [unite(b[width:], heads) for b in blocks]
    top = functools.reduce(jnp.maximum, lses)
    shares = [jnp.exp(x - top) for x in lses]
    total = sum(shares)
    shares = [x / total for x in shares]
    outs = []
    for h in range(heads):
        rows = slice(h * HEAD_SIZE, (h + 1) * HEAD_SIZE)
        outs.append(sum(x[h : h + 1] * b[rows].astype(jnp.float32) for b, x in zip(blocks, shares)))
    return jnp.concatenate(outs, axis=0), top + jnp.log(total)


def merge_pair_kernel(a_ref, b_ref, *out_refs):
    for k, out_ref in enumerate(out_refs):
        out, lse = merge([a_ref[k], b_ref[k]])
        width = out.shape[0]
        out_ref[:width, :] = out.astype(jnp.bfloat16)
        out_ref[width:, :] = thirds(lse)


def merge_final_kernel(count, *refs):
    grad_ref, context_ref, stats_ref = refs[count:]
    out, lse = merge([r[...] for r in refs[:count]])
    context = out.T.astype(jnp.bfloat16)
    context_ref[...] = context
    product = (context.astype(jnp.float32) * grad_ref[...].astype(jnp.float32)).T
    dots = [
        jnp.sum(product[h * HEAD_SIZE : (h + 1) * HEAD_SIZE], axis=0, keepdims=True) for h in range(lse.shape[0])
    ]
    stats_ref[...] = jnp.concatenate([lse] + dots, axis=0)


def backward_kernel(slots, carried, passages, me_ref, lengths_ref, *refs):
    count = len(slots)
    q_refs, g_refs, stats_refs = refs[:count], refs[count : 2 * count], refs[2 * count : 3 * count]
    keys_ref, values_ref = refs[3 * count : 3 * count + 2]
    (dk_ref, dv_ref, even_ref, odd_ref, q_buf, g_buf, st_buf, k_buf, v_buf, dk_buf, dv_buf, bias_ref, sem) = refs[
        3 * count + 2 + carried :
    ]
    me = me_ref[0]
    width = q_buf.shape[2]
    first = slots[0]

    def k_copy(i):
        return pltpu.make_async_copy(columns_of(keys_ref, me, first + i, width), k_buf.at[i], sem.at[0, i])

    def v_copy(i):
        return pltpu.make_async_copy(columns_of(values_ref, me, first + i, width), v_buf.at[i], sem.at[1, i])

    def dk_copy(i):
        return pltpu.make_async_copy(dk_buf.at[i], columns_of(dk_ref, me, first + i, width), sem.at[2, i])

    def dv_copy(i):
        return pltpu.make_async_copy(dv_buf.at[i], columns_of(dv_ref, me, first + i, width), sem.at[3, i])

    for i in range(count):
        k_copy(i).start()
        v_copy(i).start()
    for i in range(count):
        q_buf[i] = q_refs[i][...]
        g_buf[i] = g_refs[i][...]
        st_buf[i] = stats_refs[i][...]
    bias_ref[...] = mask_bias(lengths_ref, passages, k_buf.shape[1] // passages)
    lane_low = lax.broadcasted_iota(jnp.int32, (1, PAIR), 1) < HEAD_SIZE
    heads = width // HEAD_SIZE

    def one_slot(i, out_ref, k):
        k_copy(i).wait()
        v_copy(i).wait()
        for p in range(width // PAIR):
            lanes = slice(p * PAIR, (p + 1) * PAIR)
            queries = block_stack(q_buf[i, :, lanes], lane_low)
            grads = block_stack(g_buf[i, :, lanes], lane_low)
            stats = st_buf[i]
            lse = jnp.concatenate([stats[2 * p : 2 * p + 1], stats[2 * p + 1 : 2 * p + 2]], axis=1)
            dots = jnp.concatenate(
                [stats[heads + 2 * p : heads + 2 * p + 1], stats[heads + 2 * p + 1 : heads + 2 * p + 2]], axis=1
            )
            key_block = k_buf[i, :, lanes]
            bias = bias_ref[...]
            scores = dot(key_block, queries, NT) + jnp.concatenate([bias, bias], axis=1)
            probs = jnp.exp(scores - lse)
            prob_grad = dot(v_buf[i, :, lanes], grads, NT)
            score_grad = (probs * (prob_grad - dots)).astype(jnp.bfloat16)
            dv_buf[i, :, lanes] = dot(probs.astype(jnp.bfloat16), grads, NN).astype(jnp.bfloat16)
            dk_buf[i, :, lanes] = dot(score_grad, queries, NN).astype(jnp.bfloat16)
            out_ref[k, lanes, :] = diagonal(dot(key_block, score_grad, TN)).astype(jnp.bfloat16)
        dk_copy(i).start()
        dv_copy(i).start()

    def body(k, carry):
        one_slot(2 * k, even_ref, k)
        one_slot(2 * k + 1, odd_ref, k)
        return carry

    lax.fori_loop(0, count // 2, body, 0)
    for i in range(count):
        dk_copy(i).wait()
        dv_copy(i).wait()


def add_pair_kernel(a_ref, b_ref, *out_refs):
    for k, out_ref in enumerate(out_refs):
        out_ref[...] = (a_ref[k].astype(jnp.float32) + b_ref[k].astype(jnp.float32)).astype(jnp.bfloat16)


def add_all_kernel(*refs):
    total = refs[0][...].astype(jnp.float32)
    for r in refs[1:-1]:
        total += r[...].astype(jnp.float32)
    refs[-1][...] = total.astype(jnp.bfloat16)


def add_all_transposed_kernel(*refs):
    total = refs[0][...].astype(jnp.float32)
    for r in refs[1:-1]:
        total += r[...].astype(jnp.float32)
    refs[-1][...] = total.T.astype(jnp.bfloat16)


def grad_partial_kernel(size, me_ref, cot_ref, weight_ref, even_ref, odd_ref, w_buf, sem):
    me = me_ref[0]
    width = w_buf.shape[2]

    def w_copy(s):
        return pltpu.make_async_copy(columns_of(weight_ref, me, s, width), w_buf.at[s], sem.at[s])

    order = list(range(1, size, 2)) + list(range(0, size, 2))
    for s in order:
        w_copy(s).start()
    cot = cot_ref[...]
    for s in order:
        w_copy(s).wait()
        (odd_ref if s % 2 else even_ref)[s // 2] = dot(cot, w_buf[s], NN).astype(jnp.bfloat16)


def layer_out_kernel(size, me_ref, *refs):
    weight_ref, out_ref, w_buf, sem = refs[size:]
    me = me_ref[0]
    width = w_buf.shape[2]

    def w_copy(s):
        return pltpu.make_async_copy(columns_of(weight_ref, me, s, width), w_buf.at[s], sem.at[s])

    for s in range(size):
        w_copy(s).start()
    total = None
    for s in range(size):
        w_copy(s).wait()
        part = dot(refs[s][...], w_buf[s], NT)
        total = part if total is None else total + part
    out_ref[...] = total.astype(jnp.bfloat16)


def weight_grad_kernel(size, groups, me_ref, *refs):
    half = size // 2
    cots = refs[:groups]
    own_even, own_odd = refs[groups : groups + half], refs[groups + half : groups + size]
    rest = refs[groups + size :]
    evens, odds = rest[: groups - 1], rest[groups - 1 : 2 * (groups - 1)]
    out_ref, cot_buf, out_buf, sem = rest[2 * (groups - 1) :]
    me = me_ref[0]
    width = out_buf.shape[2]
    rows = cots[0].shape[0]
    for g in range(groups):
        cot_buf[:, g * rows : (g + 1) * rows] = cots[g][...].T

    def out_copy(s):
        return pltpu.make_async_copy(out_buf.at[s], columns_of(out_ref, me, s, width), sem.at[s])

    for s in range(size):
        own, others = (own_odd, odds) if s % 2 else (own_even, evens)
        context = jnp.concatenate([own[s // 2][...]] + [o[s // 2] for o in others], axis=0)
        out_buf[s] = dot(cot_buf[...], context, NN)
        out_copy(s).start()
    for s in range(size):
        out_copy(s).wait()


def stack_kernel(*refs):
    for k, r in enumerate(refs[:-1]):
        refs[-1][k] = r[...]


def shaped(shape, dtype):
    return jax.ShapeDtypeStruct(shape, dtype)


def fast_device(dp, size, queries, keys, values, lengths, out_weight, out_cotangent):
    bf16, f32 = jnp.bfloat16, jnp.float32
    passages, passage_len, inner = keys.shape[1:]
    key_count = passages * passage_len
    answers, width = queries.shape[1:]
    half = size // 2
    heads = width // HEAD_SIZE
    model = out_weight.shape[0]
    me = lax.axis_index("psg").reshape(1)
    query = queries[0]
    cot = out_cotangent[0]
    key_rows = keys.reshape(key_count, inner)
    value_rows = values.reshape(key_count, inner)

    def interleaved(even, odd):
        return [r for pair in zip(even, odd) for r in pair]

    q_even = spread(query, size)
    slots = interleaved(q_even, across(q_even, size))
    cots = [cot] + [swap(cot, "dp", dp, d) for d in range(1, dp)]

    g_even, g_odd = call(
        functools.partial(grad_partial_kernel, size),
        me,
        cot,
        out_weight,
        out=[shaped((half, answers, width), bf16)] * 2,
        ins=[SMEM, VMEM, ANY],
        outs=[VMEM, VMEM],
        scratch=[pltpu.VMEM((size, model, width), bf16), pltpu.SemaphoreType.DMA((size,))],
    )
    g_other = swap(g_odd, "psg", size, 1)
    block = shaped((answers, width), bf16)
    g_sums = call(add_pair_kernel, g_even, g_other, out=[block] * half, ins=[VMEM] * 2, outs=[VMEM] * half)
    g_parts = [swap(g_sums[d // 2], "psg", size, d) for d in far_first(size)]

    packed = shaped((width + EXTRA, answers), bf16)
    o_even, o_odd = call(
        functools.partial(forward_kernel, size, passages),
        me,
        lengths,
        *slots,
        key_rows,
        value_rows,
        out=[shaped((half, width + EXTRA, answers), bf16)] * 2,
        ins=[SMEM, SMEM] + [VMEM] * size + [ANY, ANY],
        outs=[VMEM] * 2,
        scratch=[
            pltpu.VMEM((size, answers, width), bf16),
            pltpu.VMEM((size, key_count, width), bf16),
            pltpu.VMEM((size, key_count, width), bf16),
            pltpu.VMEM((key_count, PAIR), f32),
            pltpu.SemaphoreType.DMA((2, size)),
        ],
        vmem=16,
    )

    o_other = swap(o_odd, "psg", size, 1)
    o_pairs = call(merge_pair_kernel, o_even, o_other, out=[packed] * half, ins=[VMEM] * 2, outs=[VMEM] * half)
    arrived = [swap(o_pairs[d // 2], "psg", size, d) for d in far_first(size)]
    context_grad = call(add_all_kernel, g_sums[0], *g_parts, out=block, ins=[VMEM] * half, outs=VMEM)
    cg_even = spread(context_grad, size)
    context, stats = call(
        functools.partial(merge_final_kernel, half),
        o_pairs[0],
        *arrived,
        context_grad,
        out=[block, shaped((2 * heads, answers), f32)],
        ins=[VMEM] * (half + 1),
        outs=[VMEM] * 2,
    )
    s_even = spread(stats, size)
    c_even = spread(context, size)
    g_slots = interleaved(cg_even, across(cg_even, size))
    s_slots = interleaved(s_even, across(s_even, size))

    def backward(chosen, carried):
        count = len(chosen)
        pick = slice(chosen[0], chosen[0] + count)
        fixed = 2 + 3 * count + 2
        return call(
            functools.partial(backward_kernel, chosen, len(carried), passages),
            me,
            lengths,
            *slots[pick],
            *g_slots[pick],
            *s_slots[pick],
            key_rows,
            value_rows,
            *carried,
            out=[shaped((key_count, inner), bf16)] * 2 + [shaped((count // 2, width, answers), bf16)] * 2,
            ins=[SMEM, SMEM] + [VMEM] * (3 * count) + [ANY] * (2 + len(carried)),
            outs=[ANY, ANY, VMEM, VMEM],
            scratch=[
                pltpu.VMEM((count, answers, width), bf16),
                pltpu.VMEM((count, answers, width), bf16),
                pltpu.VMEM((count, 2 * heads, answers), f32),
            ]
            + [pltpu.VMEM((count, key_count, width), bf16)] * 4
            + [pltpu.VMEM((key_count, PAIR), f32), pltpu.SemaphoreType.DMA((4, count))],
            vmem=16,
            alias={fixed + i: i for i in range(len(carried))},
        )

    def owners_sums(even, odd, count):
        other = swap(odd, "psg", size, 1)
        return call(
            add_pair_kernel,
            even,
            other,
            out=[shaped((width, answers), bf16)] * count,
            ins=[VMEM] * 2,
            outs=[VMEM] * count,
        )

    key_grad, value_grad, far_even, far_odd = backward(range(half, size), ())
    far_sums = owners_sums(far_even, far_odd, half // 2)
    key_grad, value_grad, near_even, near_odd = backward(range(half), (key_grad, value_grad))
    near_sums = owners_sums(near_even, near_odd, half // 2)
    sums = near_sums + far_sums
    dq_parts = [swap(sums[d // 2], "psg", size, d) for d in far_first(size)]
    query_grad = call(add_all_transposed_kernel, sums[0], *dq_parts, out=block, ins=[VMEM] * half, outs=VMEM)

    c_odd = across(c_even, size)
    stacked = call(stack_kernel, *c_even, out=shaped((half, answers, width), bf16), ins=[VMEM] * half, outs=VMEM)
    evens = [swap(stacked, "dp", dp, d) for d in range(1, dp)]
    odds = [swap(e, "psg", size, 1) for e in evens]
    layer_out = call(
        functools.partial(layer_out_kernel, size),
        me,
        *interleaved(c_even, c_odd),
        out_weight,
        out=shaped((answers, model), bf16),
        ins=[SMEM] + [VMEM] * size + [ANY],
        outs=VMEM,
        scratch=[pltpu.VMEM((size, model, width), bf16), pltpu.SemaphoreType.DMA((size,))],
    )
    weight_grad = call(
        functools.partial(weight_grad_kernel, size, dp),
        me,
        *cots,
        *c_even,
        *c_odd,
        *evens,
        *odds,
        out=shaped((model, inner), f32),
        ins=[SMEM] + [VMEM] * (dp + size + 2 * (dp - 1)),
        outs=ANY,
        scratch=[
            pltpu.VMEM((model, dp * answers), bf16),
            pltpu.VMEM((size, model, width), f32),
            pltpu.SemaphoreType.DMA((size,)),
        ],
        vmem=16,
    )
    return (
        layer_out[None],
        weight_grad,
        query_grad[None],
        key_grad.reshape(keys.shape),
        value_grad.reshape(values.shape),
    )


def spread_heads(factor):
    return jnp.transpose(factor, (0, 2, 1))[..., None]


def general_device(queries, keys, values, lengths, out_weight, out_cotangent):
    question_count, passages, passage_len, inner_dim = keys.shape
    key_count = passages * passage_len
    answer_len = queries.shape[1]
    head_split = (question_count, answer_len, inner_dim // HEAD_SIZE, HEAD_SIZE)
    key_split = (question_count, key_count, inner_dim // HEAD_SIZE, HEAD_SIZE)
    einsum = functools.partial(jnp.einsum, preferred_element_type=jnp.float32)
    query_heads = lax.all_gather(queries, "psg", axis=2, tiled=True).reshape(head_split)
    key_heads = keys.reshape(key_split)
    value_heads = values.reshape(key_split)
    positions = jnp.arange(passage_len, dtype=jnp.int32)
    valid = (positions[None, None, :] < lengths[:, :, None]).reshape(question_count, 1, 1, key_count)
    scores = einsum("bihe,bkhe->bhik", query_heads, key_heads)
    row_max = lax.pmax(jnp.max(jnp.where(valid, scores, -jnp.inf), axis=3), "psg")
    weights = jnp.where(valid, jnp.exp(scores - row_max[..., None]), 0.0)
    output = einsum("bhik,bkhe->bihe", weights.astype(jnp.bfloat16), value_heads)
    row_sum, output = lax.psum((jnp.sum(weights, axis=3), output), "psg")
    context = (output / spread_heads(row_sum)).astype(jnp.bfloat16)
    context_rows = context.reshape(question_count * answer_len, inner_dim)
    grad_rows = out_cotangent.reshape(question_count * answer_len, -1)
    layer_out = jnp.dot(context_rows, out_weight.T, preferred_element_type=jnp.float32).astype(jnp.bfloat16)
    weight_grad = lax.psum(
        jnp.dot(grad_rows.T, context_rows, preferred_element_type=jnp.float32).astype(jnp.bfloat16), "dp"
    ).astype(jnp.float32)
    context_grad = lax.psum(jnp.dot(grad_rows, out_weight, preferred_element_type=jnp.float32), "psg").astype(
        jnp.bfloat16
    )
    grad_heads = context_grad.reshape(head_split)
    products = grad_heads.astype(jnp.float32) * context.astype(jnp.float32)
    row_dots = jnp.transpose(jnp.sum(products, axis=3), (0, 2, 1))
    probs = weights / row_sum[..., None]
    prob_grad = einsum("bihe,bkhe->bhik", grad_heads, value_heads)
    score_grad = (probs * (prob_grad - row_dots[..., None])).astype(jnp.bfloat16)
    value_grad = einsum("bhik,bihe->bkhe", probs.astype(jnp.bfloat16), grad_heads)
    key_grad = einsum("bhik,bihe->bkhe", score_grad, query_heads)
    query_terms = einsum("bhik,bkhe->bihe", score_grad, key_heads).reshape(question_count, answer_len, inner_dim)
    query_grad = lax.psum_scatter(query_terms, "psg", scatter_dimension=2, tiled=True)
    return (
        layer_out.reshape(question_count, answer_len, -1),
        weight_grad,
        query_grad.astype(jnp.bfloat16),
        key_grad.astype(jnp.bfloat16).reshape(keys.shape),
        value_grad.astype(jnp.bfloat16).reshape(values.shape),
    )


def solution(mesh):
    dp, size = mesh.shape["dp"], mesh.shape["psg"]

    def per_device(queries, keys, values, lengths, out_weight, out_cotangent):
        return fast_device(dp, size, queries, keys, values, lengths, out_weight, out_cotangent)

    def step(queries, keys, values, lengths, out_weight, out_cotangent):
        width = queries.shape[2] // size
        direct = (
            size in (4, 8)
            and dp in (2, 4)
            and keys.shape[0] == dp
            and width % PAIR == 0
            and 3 * (width // HEAD_SIZE) <= EXTRA
            and 2 * (width // HEAD_SIZE) % 8 == 0
            and queries.shape[1] % 128 == 0
            and keys.shape[2] % 16 == 0
            and (out_weight.shape[0] // size) % 128 == 0
        )
        body = jax.shard_map(
            per_device if direct else general_device,
            mesh=mesh,
            in_specs=(
                P("dp", None, "psg"),
                P("dp", "psg", None, None),
                P("dp", "psg", None, None),
                P("dp", "psg"),
                P("psg", None),
                P("dp", None, "psg"),
            ),
            out_specs=(
                P("dp", None, "psg"),
                P("psg", None),
                P("dp", None, "psg"),
                P("dp", "psg", None, None),
                P("dp", "psg", None, None),
            ),
            check_vma=False,
        )
        return body(queries, keys, values, lengths, out_weight, out_cotangent)

    return step
```

```python
import functools

import jax
import jax.numpy as jnp
from jax import lax
from jax.experimental import pallas as pl
from jax.experimental.pallas import tpu as pltpu
from jax.sharding import PartitionSpec as P

HEAD_SIZE = 64
PAIR = 2 * HEAD_SIZE
MASKED = -1e30
EXTRA = 16
MIB = 1 << 20

NT = (((1,), (1,)), ((), ()))
NN = (((1,), (0,)), ((), ()))
TN = (((0,), (0,)), ((), ()))
ANY = pl.BlockSpec(memory_space=pl.ANY)
VMEM = pl.BlockSpec(memory_space=pltpu.VMEM)
SMEM = pl.BlockSpec(memory_space=pltpu.SMEM)
HBM = pl.BlockSpec(memory_space=pltpu.HBM)


def dot(a, b, dims):
    return lax.dot_general(a, b, dims, preferred_element_type=jnp.float32)


def swap(x, axis, size, distance):
    return lax.ppermute(x, axis, [(j, j ^ distance) for j in range(size)])


def call(kernel, *args, out, ins, outs, scratch=(), vmem=8, alias=None):
    return pl.pallas_call(
        kernel,
        out_shape=out,
        in_specs=ins,
        out_specs=outs,
        scratch_shapes=list(scratch),
        input_output_aliases=alias or {},
        compiler_params=pltpu.CompilerParams(vmem_limit_bytes=vmem * MIB),
    )(*args)


def far_first(size):
    return range(size - 2, 0, -2)


def spread(x, size):
    even = [x] + [None] * (size // 2 - 1)
    for d in far_first(size):
        even[d // 2] = swap(x, "psg", size, d)
    return even


def across(blocks, size):
    return [swap(b, "psg", size, 1) for b in blocks]


def block_stack(x, lane_low):
    zero = jnp.zeros_like(x)
    return jnp.concatenate([jnp.where(lane_low, x, zero), jnp.where(lane_low, zero, x)], axis=0)


def diagonal(x):
    rows = x.shape[1] // 2
    return jnp.concatenate([x[:HEAD_SIZE, :rows], x[HEAD_SIZE:, rows:]], axis=0)


def mask_bias(lengths_ref, passages, passage_len):
    row = lax.broadcasted_iota(jnp.int32, (passage_len, PAIR), 0)
    return jnp.concatenate([jnp.where(row < lengths_ref[0, p], 0.0, MASKED) for p in range(passages)], axis=0)


def split3(x):
    high = x.astype(jnp.bfloat16).astype(jnp.float32)
    middle = (x - high).astype(jnp.bfloat16).astype(jnp.float32)
    return high, middle, (x - high - middle).astype(jnp.bfloat16).astype(jnp.float32)


def thirds(x):
    pad = jnp.zeros((EXTRA - 3 * x.shape[0], x.shape[1]), jnp.float32)
    return jnp.concatenate([*split3(x), pad], axis=0).astype(jnp.bfloat16)


def unite(rows, heads):
    wide = rows.astype(jnp.float32)
    return wide[:heads] + wide[heads : 2 * heads] + wide[2 * heads : 3 * heads]


def columns_of(ref, me, slot, width):
    owner = jnp.bitwise_xor(me, slot)
    return ref.at[:, pl.ds(pl.multiple_of(owner * width, width), width)]


def forward_kernel(size, passages, lengths_ref, *refs):
    q_refs = refs[:size]
    keys_ref, values_ref, even_ref, odd_ref, q_buf, bias_ref = refs[size:]
    width = q_buf.shape[2]
    for s in range(size):
        q_buf[s] = q_refs[s][...]
    bias_ref[...] = mask_bias(lengths_ref, passages, keys_ref.shape[1] // passages)
    lane_low = lax.broadcasted_iota(jnp.int32, (1, PAIR), 1) < HEAD_SIZE

    def one_slot(s, out_ref, k):
        rows = []
        for p in range(width // PAIR):
            lanes = slice(p * PAIR, (p + 1) * PAIR)
            queries = block_stack(q_buf[s, :, lanes], lane_low)
            bias = bias_ref[...]
            scores = dot(keys_ref[s, :, lanes], queries, NT) + jnp.concatenate([bias, bias], axis=1)
            top = jnp.max(scores, axis=0, keepdims=True)
            weights = jnp.exp(scores - top)
            total = jnp.sum(weights, axis=0, keepdims=True)
            mixed = dot(values_ref[s, :, lanes], weights.astype(jnp.bfloat16), TN) / total
            out_ref[k, lanes, :] = diagonal(mixed).astype(jnp.bfloat16)
            lse = top + jnp.log(total)
            n = lse.shape[1] // 2
            rows += [lse[:, :n], lse[:, n:]]
        out_ref[k, width:, :] = thirds(jnp.concatenate(rows, axis=0))

    def body(k, carry):
        one_slot(2 * k, even_ref, k)
        one_slot(2 * k + 1, odd_ref, k)
        return carry

    lax.fori_loop(0, size // 2, body, 0)


def merge(blocks):
    width = blocks[0].shape[0] - EXTRA
    heads = width // HEAD_SIZE
    lses = [unite(b[width:], heads) for b in blocks]
    top = functools.reduce(jnp.maximum, lses)
    shares = [jnp.exp(x - top) for x in lses]
    total = sum(shares)
    shares = [x / total for x in shares]
    outs = []
    for h in range(heads):
        rows = slice(h * HEAD_SIZE, (h + 1) * HEAD_SIZE)
        outs.append(sum(x[h : h + 1] * b[rows].astype(jnp.float32) for b, x in zip(blocks, shares)))
    return jnp.concatenate(outs, axis=0), top + jnp.log(total)


def merge_pair_kernel(a_ref, b_ref, *out_refs):
    for k, out_ref in enumerate(out_refs):
        out, lse = merge([a_ref[k], b_ref[k]])
        width = out.shape[0]
        out_ref[:width, :] = out.astype(jnp.bfloat16)
        out_ref[width:, :] = thirds(lse)


def merge_final_kernel(count, *refs):
    grad_ref, out_ref = refs[count:]
    out, lse = merge([r[...] for r in refs[:count]])
    context = out.T.astype(jnp.bfloat16)
    answers, _ = context.shape
    out_ref[:answers, :] = context
    product = (context.astype(jnp.float32) * grad_ref[...].astype(jnp.float32)).T
    dots = [
        jnp.sum(product[h * HEAD_SIZE : (h + 1) * HEAD_SIZE], axis=0, keepdims=True) for h in range(lse.shape[0])
    ]
    high, middle, low = split3(jnp.concatenate([lse] + dots, axis=0))
    top = jnp.concatenate([high, middle], axis=1)
    bottom = jnp.concatenate([low, jnp.zeros_like(low)], axis=1)
    out_ref[answers:, :] = jnp.concatenate([top, bottom], axis=0).astype(jnp.bfloat16)


def stats_of(block_ref, answers):
    rows = block_ref[answers:, :].astype(jnp.float32)
    n = rows.shape[0] // 2
    return rows[:n, :answers] + rows[:n, answers:] + rows[n:, :answers]


def backward_kernel(slots, carried, passages, me_ref, lengths_ref, *refs):
    count = len(slots)
    q_refs, g_refs, c_refs = refs[:count], refs[count : 2 * count], refs[2 * count : 3 * count]
    keys_ref, values_ref = refs[3 * count : 3 * count + 2]
    dk_ref, dv_ref, even_ref, odd_ref, q_buf, g_buf, st_buf, dk_buf, dv_buf, bias_ref, sem = refs[
        3 * count + 2 + carried :
    ]
    me = me_ref[0]
    answers, width = q_buf.shape[1:]
    first = slots[0]

    def dk_copy(i):
        return pltpu.make_async_copy(dk_buf.at[i], columns_of(dk_ref, me, first + i, width), sem.at[0, i])

    def dv_copy(i):
        return pltpu.make_async_copy(dv_buf.at[i], columns_of(dv_ref, me, first + i, width), sem.at[1, i])

    for i in range(count):
        q_buf[i] = q_refs[i][...]
        g_buf[i] = g_refs[i][...]
        st_buf[i] = stats_of(c_refs[i], answers)
    bias_ref[...] = mask_bias(lengths_ref, passages, keys_ref.shape[1] // passages)
    lane_low = lax.broadcasted_iota(jnp.int32, (1, PAIR), 1) < HEAD_SIZE
    heads = width // HEAD_SIZE

    def one_slot(i, out_ref, k):
        for p in range(width // PAIR):
            lanes = slice(p * PAIR, (p + 1) * PAIR)
            queries = block_stack(q_buf[i, :, lanes], lane_low)
            grads = block_stack(g_buf[i, :, lanes], lane_low)
            stats = st_buf[i]
            lse = jnp.concatenate([stats[2 * p : 2 * p + 1], stats[2 * p + 1 : 2 * p + 2]], axis=1)
            dots = jnp.concatenate(
                [stats[heads + 2 * p : heads + 2 * p + 1], stats[heads + 2 * p + 1 : heads + 2 * p + 2]], axis=1
            )
            key_block = keys_ref[first + i, :, lanes]
            bias = bias_ref[...]
            scores = dot(key_block, queries, NT) + jnp.concatenate([bias, bias], axis=1)
            probs = jnp.exp(scores - lse)
            prob_grad = dot(values_ref[first + i, :, lanes], grads, NT)
            score_grad = (probs * (prob_grad - dots)).astype(jnp.bfloat16)
            dv_buf[i, :, lanes] = dot(probs.astype(jnp.bfloat16), grads, NN).astype(jnp.bfloat16)
            dk_buf[i, :, lanes] = dot(score_grad, queries, NN).astype(jnp.bfloat16)
            out_ref[k, lanes, :] = diagonal(dot(key_block, score_grad, TN)).astype(jnp.bfloat16)
        dk_copy(i).start()
        dv_copy(i).start()

    def body(k, carry):
        one_slot(2 * k, even_ref, k)
        one_slot(2 * k + 1, odd_ref, k)
        return carry

    lax.fori_loop(0, count // 2, body, 0)
    for i in range(count):
        dk_copy(i).wait()
        dv_copy(i).wait()


def add_pair_kernel(a_ref, b_ref, *out_refs):
    for k, out_ref in enumerate(out_refs):
        out_ref[...] = (a_ref[k].astype(jnp.float32) + b_ref[k].astype(jnp.float32)).astype(jnp.bfloat16)


def add_all_kernel(*refs):
    total = refs[0][...].astype(jnp.float32)
    for r in refs[1:-1]:
        total += r[...].astype(jnp.float32)
    refs[-1][...] = total.astype(jnp.bfloat16)


def add_all_transposed_kernel(*refs):
    total = refs[0][...].astype(jnp.float32)
    for r in refs[1:-1]:
        total += r[...].astype(jnp.float32)
    refs[-1][...] = total.T.astype(jnp.bfloat16)


def grad_partial_kernel(size, me_ref, cot_ref, weight_ref, keys_ref, values_ref, *refs):
    even_ref, odd_ref, k_out, v_out, cot_buf, w_buf, sem, cot_sem = refs
    me = me_ref[0]
    width = w_buf.shape[2]

    def copy(ref, buf, lane, s):
        return pltpu.make_async_copy(columns_of(ref, me, s, width), buf.at[s], sem.at[lane, s])

    order = list(range(1, size, 2)) + list(range(0, size, 2))
    cot_copy = pltpu.make_async_copy(cot_ref, cot_buf, cot_sem)
    cot_copy.start()
    for s in order:
        copy(weight_ref, w_buf, 0, s).start()
    for s in range(size):
        copy(keys_ref, k_out, 1, s).start()
        copy(values_ref, v_out, 2, s).start()
    cot_copy.wait()
    cot = cot_buf[...]
    for s in order:
        copy(weight_ref, w_buf, 0, s).wait()
        (odd_ref if s % 2 else even_ref)[s // 2] = dot(cot, w_buf[s], NN).astype(jnp.bfloat16)
    for s in range(size):
        copy(keys_ref, k_out, 1, s).wait()
        copy(values_ref, v_out, 2, s).wait()


def layer_out_kernel(size, me_ref, *refs):
    weight_ref, out_ref, w_buf, sem = refs[size:]
    me = me_ref[0]
    width = w_buf.shape[2]
    answers = out_ref.shape[0]

    def w_copy(s):
        return pltpu.make_async_copy(columns_of(weight_ref, me, s, width), w_buf.at[s], sem.at[s])

    for s in range(size):
        w_copy(s).start()
    total = None
    for s in range(size):
        w_copy(s).wait()
        part = dot(refs[s][:answers, :], w_buf[s], NT)
        total = part if total is None else total + part
    out_ref[...] = total.astype(jnp.bfloat16)


def weight_grad_kernel(size, groups, answers, me_ref, *refs):
    half = size // 2
    packs, packs_odd, own = refs[:groups], refs[groups : 2 * groups - 1], refs[2 * groups - 1 : 2 * groups - 1 + half]
    out_ref, cot_buf, out_buf, sem = refs[2 * groups - 1 + half :]
    me = me_ref[0]
    width = out_buf.shape[2]
    for g in range(groups):
        for r in range(cot_buf.shape[0] // width):
            cot_buf[r * width : (r + 1) * width, g * answers : (g + 1) * answers] = packs[g][half + r].T

    def out_copy(s):
        return pltpu.make_async_copy(out_buf.at[s], columns_of(out_ref, me, s, width), sem.at[s])

    for s in range(size):
        k = s // 2
        if s % 2:
            blocks = [own[k][:answers, :]] + [o[k] for o in packs_odd]
        else:
            blocks = [o[k] for o in packs]
        out_buf[s] = dot(cot_buf[...], jnp.concatenate(blocks, axis=0), NN)
        out_copy(s).start()
    for s in range(size):
        out_copy(s).wait()


def pack_kernel(half, cot_ref, *refs):
    out_ref = refs[half]
    answers, width = out_ref.shape[1:]
    for k in range(half):
        out_ref[k] = refs[k][:answers, :]
    for r in range(cot_ref.shape[1] // width):
        out_ref[half + r] = cot_ref[:, r * width : (r + 1) * width]


def shaped(shape, dtype):
    return jax.ShapeDtypeStruct(shape, dtype)


def fast_device(dp, size, queries, keys, values, lengths, out_weight, out_cotangent):
    bf16, f32 = jnp.bfloat16, jnp.float32
    passages, passage_len, inner = keys.shape[1:]
    key_count = passages * passage_len
    answers, width = queries.shape[1:]
    half = size // 2
    heads = width // HEAD_SIZE
    model = out_weight.shape[0]
    me = lax.axis_index("psg").reshape(1)
    query = queries[0]
    cot = out_cotangent[0]
    key_rows = keys.reshape(key_count, inner)
    value_rows = values.reshape(key_count, inner)

    def interleaved(even, odd):
        return [r for pair in zip(even, odd) for r in pair]

    q_even = spread(query, size)
    slots = interleaved(q_even, across(q_even, size))

    resident = shaped((size, key_count, width), bf16)
    g_even, g_odd, slot_keys, slot_values = call(
        functools.partial(grad_partial_kernel, size),
        me,
        cot,
        out_weight,
        key_rows,
        value_rows,
        out=[shaped((half, answers, width), bf16)] * 2 + [resident] * 2,
        ins=[SMEM] + [HBM] * 4,
        outs=[VMEM] * 4,
        scratch=[
            pltpu.VMEM((answers, model), bf16),
            pltpu.VMEM((size, model, width), bf16),
            pltpu.SemaphoreType.DMA((3, size)),
            pltpu.SemaphoreType.DMA(()),
        ],
        vmem=12,
    )
    g_other = swap(g_odd, "psg", size, 1)
    block = shaped((answers, width), bf16)
    g_sums = call(add_pair_kernel, g_even, g_other, out=[block] * half, ins=[VMEM] * 2, outs=[VMEM] * half)
    g_parts = [swap(g_sums[d // 2], "psg", size, d) for d in far_first(size)]

    packed = shaped((width + EXTRA, answers), bf16)
    o_even, o_odd = call(
        functools.partial(forward_kernel, size, passages),
        lengths,
        *slots,
        slot_keys,
        slot_values,
        out=[shaped((half, width + EXTRA, answers), bf16)] * 2,
        ins=[SMEM] + [VMEM] * (size + 2),
        outs=[VMEM] * 2,
        scratch=[pltpu.VMEM((size, answers, width), bf16), pltpu.VMEM((key_count, PAIR), f32)],
        vmem=16,
    )

    o_other = swap(o_odd, "psg", size, 1)
    o_pairs = call(merge_pair_kernel, o_even, o_other, out=[packed] * half, ins=[VMEM] * 2, outs=[VMEM] * half)
    arrived = [swap(o_pairs[d // 2], "psg", size, d) for d in far_first(size)]
    context_grad = call(add_all_kernel, g_sums[0], *g_parts, out=block, ins=[VMEM] * half, outs=VMEM)
    cg_even = spread(context_grad, size)
    context = call(
        functools.partial(merge_final_kernel, half),
        o_pairs[0],
        *arrived,
        context_grad,
        out=shaped((answers + 4 * heads, width), bf16),
        ins=[VMEM] * (half + 1),
        outs=VMEM,
    )
    c_even = spread(context, size)
    c_odd = across(c_even, size)
    c_slots = interleaved(c_even, c_odd)
    g_slots = interleaved(cg_even, across(cg_even, size))

    def backward(chosen, carried):
        count = len(chosen)
        pick = slice(chosen[0], chosen[0] + count)
        fixed = 2 + 3 * count + 2
        return call(
            functools.partial(backward_kernel, chosen, len(carried), passages),
            me,
            lengths,
            *slots[pick],
            *g_slots[pick],
            *c_slots[pick],
            slot_keys,
            slot_values,
            *carried,
            out=[shaped((key_count, inner), bf16)] * 2 + [shaped((count // 2, width, answers), bf16)] * 2,
            ins=[SMEM, SMEM] + [VMEM] * (3 * count + 2) + [ANY] * len(carried),
            outs=[ANY, ANY, VMEM, VMEM],
            scratch=[
                pltpu.VMEM((count, answers, width), bf16),
                pltpu.VMEM((count, answers, width), bf16),
                pltpu.VMEM((count, 2 * heads, answers), f32),
            ]
            + [pltpu.VMEM((count, key_count, width), bf16)] * 2
            + [pltpu.VMEM((key_count, PAIR), f32), pltpu.SemaphoreType.DMA((2, count))],
            vmem=16,
            alias={fixed + i: i for i in range(len(carried))},
        )

    def owners_sums(even, odd, count):
        other = swap(odd, "psg", size, 1)
        return call(
            add_pair_kernel,
            even,
            other,
            out=[shaped((width, answers), bf16)] * count,
            ins=[VMEM] * 2,
            outs=[VMEM] * count,
        )

    key_grad, value_grad, far_even, far_odd = backward(range(half, size), ())
    far_sums = owners_sums(far_even, far_odd, half // 2)
    key_grad, value_grad, near_even, near_odd = backward(range(half), (key_grad, value_grad))
    near_sums = owners_sums(near_even, near_odd, half // 2)
    sums = near_sums + far_sums
    dq_parts = [swap(sums[d // 2], "psg", size, d) for d in far_first(size)]
    query_grad = call(add_all_transposed_kernel, sums[0], *dq_parts, out=block, ins=[VMEM] * half, outs=VMEM)

    pack = call(
        functools.partial(pack_kernel, half),
        cot,
        *c_even,
        out=shaped((half + model // width, answers, width), bf16),
        ins=[VMEM] * (half + 1),
        outs=VMEM,
    )
    packs = [pack] + [swap(pack, "dp", dp, d) for d in range(1, dp)]
    packs_odd = [swap(packs[d], "psg", size, 1) for d in range(1, dp)]
    layer_out = call(
        functools.partial(layer_out_kernel, size),
        me,
        *c_slots,
        out_weight,
        out=shaped((answers, model), bf16),
        ins=[SMEM] + [VMEM] * size + [ANY],
        outs=VMEM,
        scratch=[pltpu.VMEM((size, model, width), bf16), pltpu.SemaphoreType.DMA((size,))],
    )
    weight_grad = call(
        functools.partial(weight_grad_kernel, size, dp, answers),
        me,
        *packs,
        *packs_odd,
        *c_odd,
        out=shaped((model, inner), f32),
        ins=[SMEM] + [VMEM] * (2 * dp - 1 + half),
        outs=ANY,
        scratch=[
            pltpu.VMEM((model, dp * answers), bf16),
            pltpu.VMEM((size, model, width), f32),
            pltpu.SemaphoreType.DMA((size,)),
        ],
        vmem=16,
    )
    return (
        layer_out[None],
        weight_grad,
        query_grad[None],
        key_grad.reshape(keys.shape),
        value_grad.reshape(values.shape),
    )


def spread_heads(factor):
    return jnp.transpose(factor, (0, 2, 1))[..., None]


def general_device(queries, keys, values, lengths, out_weight, out_cotangent):
    question_count, passages, passage_len, inner_dim = keys.shape
    key_count = passages * passage_len
    answer_len = queries.shape[1]
    head_split = (question_count, answer_len, inner_dim // HEAD_SIZE, HEAD_SIZE)
    key_split = (question_count, key_count, inner_dim // HEAD_SIZE, HEAD_SIZE)
    einsum = functools.partial(jnp.einsum, preferred_element_type=jnp.float32)
    query_heads = lax.all_gather(queries, "psg", axis=2, tiled=True).reshape(head_split)
    key_heads = keys.reshape(key_split)
    value_heads = values.reshape(key_split)
    positions = jnp.arange(passage_len, dtype=jnp.int32)
    valid = (positions[None, None, :] < lengths[:, :, None]).reshape(question_count, 1, 1, key_count)
    scores = einsum("bihe,bkhe->bhik", query_heads, key_heads)
    row_max = lax.pmax(jnp.max(jnp.where(valid, scores, -jnp.inf), axis=3), "psg")
    weights = jnp.where(valid, jnp.exp(scores - row_max[..., None]), 0.0)
    output = einsum("bhik,bkhe->bihe", weights.astype(jnp.bfloat16), value_heads)
    row_sum, output = lax.psum((jnp.sum(weights, axis=3), output), "psg")
    context = (output / spread_heads(row_sum)).astype(jnp.bfloat16)
    context_rows = context.reshape(question_count * answer_len, inner_dim)
    grad_rows = out_cotangent.reshape(question_count * answer_len, -1)
    layer_out = jnp.dot(context_rows, out_weight.T, preferred_element_type=jnp.float32).astype(jnp.bfloat16)
    weight_grad = lax.psum(
        jnp.dot(grad_rows.T, context_rows, preferred_element_type=jnp.float32).astype(jnp.bfloat16), "dp"
    ).astype(jnp.float32)
    context_grad = lax.psum(jnp.dot(grad_rows, out_weight, preferred_element_type=jnp.float32), "psg").astype(
        jnp.bfloat16
    )
    grad_heads = context_grad.reshape(head_split)
    products = grad_heads.astype(jnp.float32) * context.astype(jnp.float32)
    row_dots = jnp.transpose(jnp.sum(products, axis=3), (0, 2, 1))
    probs = weights / row_sum[..., None]
    prob_grad = einsum("bihe,bkhe->bhik", grad_heads, value_heads)
    score_grad = (probs * (prob_grad - row_dots[..., None])).astype(jnp.bfloat16)
    value_grad = einsum("bhik,bihe->bkhe", probs.astype(jnp.bfloat16), grad_heads)
    key_grad = einsum("bhik,bihe->bkhe", score_grad, query_heads)
    query_terms = einsum("bhik,bkhe->bihe", score_grad, key_heads).reshape(question_count, answer_len, inner_dim)
    query_grad = lax.psum_scatter(query_terms, "psg", scatter_dimension=2, tiled=True)
    return (
        layer_out.reshape(question_count, answer_len, -1),
        weight_grad,
        query_grad.astype(jnp.bfloat16),
        key_grad.astype(jnp.bfloat16).reshape(keys.shape),
        value_grad.astype(jnp.bfloat16).reshape(values.shape),
    )


def solution(mesh):
    dp, size = mesh.shape["dp"], mesh.shape["psg"]

    def per_device(queries, keys, values, lengths, out_weight, out_cotangent):
        return fast_device(dp, size, queries, keys, values, lengths, out_weight, out_cotangent)

    def step(queries, keys, values, lengths, out_weight, out_cotangent):
        width = queries.shape[2] // size
        direct = (
            size in (4, 8)
            and dp in (2, 4)
            and keys.shape[0] == dp
            and width % PAIR == 0
            and 3 * (width // HEAD_SIZE) <= EXTRA
            and 2 * (width // HEAD_SIZE) % 8 == 0
            and queries.shape[1] % 128 == 0
            and keys.shape[2] % 16 == 0
            and (out_weight.shape[0] // size) % width == 0
        )
        body = jax.shard_map(
            per_device if direct else general_device,
            mesh=mesh,
            in_specs=(
                P("dp", None, "psg"),
                P("dp", "psg", None, None),
                P("dp", "psg", None, None),
                P("dp", "psg"),
                P("psg", None),
                P("dp", None, "psg"),
            ),
            out_specs=(
                P("dp", None, "psg"),
                P("psg", None),
                P("dp", None, "psg"),
                P("dp", "psg", None, None),
                P("dp", "psg", None, None),
            ),
            check_vma=False,
        )
        return body(queries, keys, values, lengths, out_weight, out_cotangent)

    return step
```

```python
import functools

import jax
import jax.numpy as jnp
from jax import lax
from jax.experimental import pallas as pl
from jax.experimental.pallas import tpu as pltpu
from jax.sharding import PartitionSpec as P

HEAD_SIZE = 64
PAIR = 2 * HEAD_SIZE
MASKED = -1e30
EXTRA = 16
MIB = 1 << 20

NT = (((1,), (1,)), ((), ()))
NN = (((1,), (0,)), ((), ()))
TN = (((0,), (0,)), ((), ()))
ANY = pl.BlockSpec(memory_space=pl.ANY)
VMEM = pl.BlockSpec(memory_space=pltpu.VMEM)
SMEM = pl.BlockSpec(memory_space=pltpu.SMEM)
HBM = pl.BlockSpec(memory_space=pltpu.HBM)


def dot(a, b, dims):
    return lax.dot_general(a, b, dims, preferred_element_type=jnp.float32)


def swap(x, axis, size, distance):
    return lax.ppermute(x, axis, [(j, j ^ distance) for j in range(size)])


def call(kernel, *args, out, ins, outs, scratch=(), vmem=8, alias=None):
    return pl.pallas_call(
        kernel,
        out_shape=out,
        in_specs=ins,
        out_specs=outs,
        scratch_shapes=list(scratch),
        input_output_aliases=alias or {},
        compiler_params=pltpu.CompilerParams(vmem_limit_bytes=vmem * MIB),
    )(*args)


def far_first(size):
    return range(size - 2, 0, -2)


def spread(x, size):
    even = [x] + [None] * (size // 2 - 1)
    for d in far_first(size):
        even[d // 2] = swap(x, "psg", size, d)
    return even


def across(blocks, size):
    return [swap(b, "psg", size, 1) for b in blocks]


def block_stack(x, lane_low):
    zero = jnp.zeros_like(x)
    return jnp.concatenate([jnp.where(lane_low, x, zero), jnp.where(lane_low, zero, x)], axis=0)


def diagonal(x):
    rows = x.shape[1] // 2
    return jnp.concatenate([x[:HEAD_SIZE, :rows], x[HEAD_SIZE:, rows:]], axis=0)


def mask_bias(lengths_ref, passages, passage_len):
    row = lax.broadcasted_iota(jnp.int32, (passage_len, PAIR), 0)
    return jnp.concatenate([jnp.where(row < lengths_ref[0, p], 0.0, MASKED) for p in range(passages)], axis=0)


def split3(x):
    high = x.astype(jnp.bfloat16).astype(jnp.float32)
    middle = (x - high).astype(jnp.bfloat16).astype(jnp.float32)
    return high, middle, (x - high - middle).astype(jnp.bfloat16).astype(jnp.float32)


def thirds(x):
    pad = jnp.zeros((EXTRA - 3 * x.shape[0], x.shape[1]), jnp.float32)
    return jnp.concatenate([*split3(x), pad], axis=0).astype(jnp.bfloat16)


def unite(rows, heads):
    wide = rows.astype(jnp.float32)
    return wide[:heads] + wide[heads : 2 * heads] + wide[2 * heads : 3 * heads]


def columns_of(ref, me, slot, width):
    owner = jnp.bitwise_xor(me, slot)
    return ref.at[:, pl.ds(pl.multiple_of(owner * width, width), width)]


def forward_kernel(size, passages, lengths_ref, *refs):
    q_refs = refs[:size]
    keys_ref, values_ref, even_ref, odd_ref, q_buf, bias_ref = refs[size:]
    width = q_buf.shape[2]
    for s in range(size):
        q_buf[s] = q_refs[s][...]
    bias_ref[...] = mask_bias(lengths_ref, passages, keys_ref.shape[1] // passages)
    lane_low = lax.broadcasted_iota(jnp.int32, (1, PAIR), 1) < HEAD_SIZE

    def one_slot(s, out_ref, k):
        rows = []
        for p in range(width // PAIR):
            lanes = slice(p * PAIR, (p + 1) * PAIR)
            queries = block_stack(q_buf[s, :, lanes], lane_low)
            bias = bias_ref[...]
            scores = dot(keys_ref[s, :, lanes], queries, NT) + jnp.concatenate([bias, bias], axis=1)
            top = jnp.max(scores, axis=0, keepdims=True)
            weights = jnp.exp(scores - top)
            total = jnp.sum(weights, axis=0, keepdims=True)
            mixed = dot(values_ref[s, :, lanes], weights.astype(jnp.bfloat16), TN) / total
            out_ref[k, lanes, :] = diagonal(mixed).astype(jnp.bfloat16)
            lse = top + jnp.log(total)
            n = lse.shape[1] // 2
            rows += [lse[:, :n], lse[:, n:]]
        out_ref[k, width:, :] = thirds(jnp.concatenate(rows, axis=0))

    def body(k, carry):
        one_slot(2 * k, even_ref, k)
        one_slot(2 * k + 1, odd_ref, k)
        return carry

    lax.fori_loop(0, size // 2, body, 0)


def merge(blocks):
    width = blocks[0].shape[0] - EXTRA
    heads = width // HEAD_SIZE
    lses = [unite(b[width:], heads) for b in blocks]
    top = functools.reduce(jnp.maximum, lses)
    shares = [jnp.exp(x - top) for x in lses]
    total = sum(shares)
    shares = [x / total for x in shares]
    outs = []
    for h in range(heads):
        rows = slice(h * HEAD_SIZE, (h + 1) * HEAD_SIZE)
        outs.append(sum(x[h : h + 1] * b[rows].astype(jnp.float32) for b, x in zip(blocks, shares)))
    return jnp.concatenate(outs, axis=0), top + jnp.log(total)


def merge_pair_kernel(a_ref, b_ref, *out_refs):
    for k, out_ref in enumerate(out_refs):
        out, lse = merge([a_ref[k], b_ref[k]])
        width = out.shape[0]
        out_ref[:width, :] = out.astype(jnp.bfloat16)
        out_ref[width:, :] = thirds(lse)


def merge_final_kernel(count, *refs):
    grad_ref, out_ref = refs[count:]
    out, lse = merge([r[...] for r in refs[:count]])
    context = out.T.astype(jnp.bfloat16)
    answers, _ = context.shape
    out_ref[:answers, :] = context
    product = (context.astype(jnp.float32) * grad_ref[...].astype(jnp.float32)).T
    dots = [
        jnp.sum(product[h * HEAD_SIZE : (h + 1) * HEAD_SIZE], axis=0, keepdims=True) for h in range(lse.shape[0])
    ]
    high, middle, low = split3(jnp.concatenate([lse] + dots, axis=0))
    top = jnp.concatenate([high, middle], axis=1)
    bottom = jnp.concatenate([low, jnp.zeros_like(low)], axis=1)
    out_ref[answers:, :] = jnp.concatenate([top, bottom], axis=0).astype(jnp.bfloat16)


def stats_of(block_ref, answers):
    rows = block_ref[answers:, :].astype(jnp.float32)
    n = rows.shape[0] // 2
    return rows[:n, :answers] + rows[:n, answers:] + rows[n:, :answers]


def backward_kernel(slots, carried, passages, me_ref, lengths_ref, *refs):
    count = len(slots)
    q_refs, g_refs, c_refs = refs[:count], refs[count : 2 * count], refs[2 * count : 3 * count]
    keys_ref, values_ref = refs[3 * count : 3 * count + 2]
    dk_ref, dv_ref, even_ref, odd_ref, q_buf, g_buf, st_buf, dk_buf, dv_buf, bias_ref, sem = refs[
        3 * count + 2 + carried :
    ]
    me = me_ref[0]
    answers, width = q_buf.shape[1:]
    first = slots[0]

    def dk_copy(i):
        return pltpu.make_async_copy(dk_buf.at[i], columns_of(dk_ref, me, first + i, width), sem.at[0, i])

    def dv_copy(i):
        return pltpu.make_async_copy(dv_buf.at[i], columns_of(dv_ref, me, first + i, width), sem.at[1, i])

    for i in range(count):
        q_buf[i] = q_refs[i][...]
        g_buf[i] = g_refs[i][...]
        st_buf[i] = stats_of(c_refs[i], answers)
    bias_ref[...] = mask_bias(lengths_ref, passages, keys_ref.shape[1] // passages)
    lane_low = lax.broadcasted_iota(jnp.int32, (1, PAIR), 1) < HEAD_SIZE
    heads = width // HEAD_SIZE

    def one_slot(i, out_ref, k):
        for p in range(width // PAIR):
            lanes = slice(p * PAIR, (p + 1) * PAIR)
            queries = block_stack(q_buf[i, :, lanes], lane_low)
            grads = block_stack(g_buf[i, :, lanes], lane_low)
            stats = st_buf[i]
            lse = jnp.concatenate([stats[2 * p : 2 * p + 1], stats[2 * p + 1 : 2 * p + 2]], axis=1)
            dots = jnp.concatenate(
                [stats[heads + 2 * p : heads + 2 * p + 1], stats[heads + 2 * p + 1 : heads + 2 * p + 2]], axis=1
            )
            key_block = keys_ref[first + i, :, lanes]
            bias = bias_ref[...]
            scores = dot(key_block, queries, NT) + jnp.concatenate([bias, bias], axis=1)
            probs = jnp.exp(scores - lse)
            prob_grad = dot(values_ref[first + i, :, lanes], grads, NT)
            score_grad = (probs * (prob_grad - dots)).astype(jnp.bfloat16)
            dv_buf[i, :, lanes] = dot(probs.astype(jnp.bfloat16), grads, NN).astype(jnp.bfloat16)
            dk_buf[i, :, lanes] = dot(score_grad, queries, NN).astype(jnp.bfloat16)
            out_ref[k, lanes, :] = diagonal(dot(key_block, score_grad, TN)).astype(jnp.bfloat16)
        dk_copy(i).start()
        dv_copy(i).start()

    def body(k, carry):
        one_slot(2 * k, even_ref, k)
        one_slot(2 * k + 1, odd_ref, k)
        return carry

    lax.fori_loop(0, count // 2, body, 0)
    for i in range(count):
        dk_copy(i).wait()
        dv_copy(i).wait()


def add_pair_kernel(a_ref, b_ref, *out_refs):
    for k, out_ref in enumerate(out_refs):
        out_ref[...] = (a_ref[k].astype(jnp.float32) + b_ref[k].astype(jnp.float32)).astype(jnp.bfloat16)


def add_all_kernel(*refs):
    total = refs[0][...].astype(jnp.float32)
    for r in refs[1:-1]:
        total += r[...].astype(jnp.float32)
    refs[-1][...] = total.astype(jnp.bfloat16)


def add_all_transposed_kernel(*refs):
    total = refs[0][...].astype(jnp.float32)
    for r in refs[1:-1]:
        total += r[...].astype(jnp.float32)
    refs[-1][...] = total.T.astype(jnp.bfloat16)


def grad_partial_kernel(size, me_ref, cot_ref, weight_ref, keys_ref, values_ref, *refs):
    even_ref, odd_ref, k_out, v_out, cot_buf, w_buf, sem, cot_sem = refs
    me = me_ref[0]
    width = w_buf.shape[2]

    def copy(ref, buf, lane, s):
        return pltpu.make_async_copy(columns_of(ref, me, s, width), buf.at[s], sem.at[lane, s])

    order = list(range(1, size, 2)) + list(range(0, size, 2))
    cot_copy = pltpu.make_async_copy(cot_ref, cot_buf, cot_sem)
    cot_copy.start()
    for s in order:
        copy(weight_ref, w_buf, 0, s).start()
    for s in range(size):
        copy(keys_ref, k_out, 1, s).start()
        copy(values_ref, v_out, 2, s).start()
    cot_copy.wait()
    cot = cot_buf[...]
    for s in order:
        copy(weight_ref, w_buf, 0, s).wait()
        (odd_ref if s % 2 else even_ref)[s // 2] = dot(cot, w_buf[s], NN).astype(jnp.bfloat16)
    for s in range(size):
        copy(keys_ref, k_out, 1, s).wait()
        copy(values_ref, v_out, 2, s).wait()


def layer_out_kernel(size, me_ref, *refs):
    weight_ref, out_ref, w_buf, sem = refs[size:]
    me = me_ref[0]
    width = w_buf.shape[2]
    answers = out_ref.shape[0]

    def w_copy(s):
        return pltpu.make_async_copy(columns_of(weight_ref, me, s, width), w_buf.at[s], sem.at[s])

    for s in range(size):
        w_copy(s).start()
    total = None
    for s in range(size):
        w_copy(s).wait()
        part = dot(refs[s][:answers, :], w_buf[s], NT)
        total = part if total is None else total + part
    out_ref[...] = total.astype(jnp.bfloat16)


def weight_grad_kernel(size, groups, answers, me_ref, *refs):
    half = size // 2
    cots, refs = refs[:groups], refs[groups:]
    packs, packs_odd, own = refs[:groups], refs[groups : 2 * groups - 1], refs[2 * groups - 1 : 2 * groups - 1 + half]
    out_ref, cot_buf, out_buf, sem = refs[2 * groups - 1 + half :]
    me = me_ref[0]
    width = out_buf.shape[2]
    for g in range(groups):
        cot_buf[:, g * answers : (g + 1) * answers] = cots[g][...].T

    def out_copy(s):
        return pltpu.make_async_copy(out_buf.at[s], columns_of(out_ref, me, s, width), sem.at[s])

    for s in range(size):
        k = s // 2
        if s % 2:
            blocks = [own[k][:answers, :]] + [o[k] for o in packs_odd]
        else:
            blocks = [o[k] for o in packs]
        out_buf[s] = dot(cot_buf[...], jnp.concatenate(blocks, axis=0), NN)
        out_copy(s).start()
    for s in range(size):
        out_copy(s).wait()


def pack_kernel(*refs):
    out_ref = refs[-1]
    for k in range(out_ref.shape[0]):
        out_ref[k] = refs[k][: out_ref.shape[1], :]


def shaped(shape, dtype):
    return jax.ShapeDtypeStruct(shape, dtype)


def fast_device(dp, size, queries, keys, values, lengths, out_weight, out_cotangent):
    bf16, f32 = jnp.bfloat16, jnp.float32
    passages, passage_len, inner = keys.shape[1:]
    key_count = passages * passage_len
    answers, width = queries.shape[1:]
    half = size // 2
    heads = width // HEAD_SIZE
    model = out_weight.shape[0]
    me = lax.axis_index("psg").reshape(1)
    query = queries[0]
    cot = out_cotangent[0]
    key_rows = keys.reshape(key_count, inner)
    value_rows = values.reshape(key_count, inner)

    def interleaved(even, odd):
        return [r for pair in zip(even, odd) for r in pair]

    q_even = spread(query, size)
    slots = interleaved(q_even, across(q_even, size))

    resident = shaped((size, key_count, width), bf16)
    g_even, g_odd, slot_keys, slot_values = call(
        functools.partial(grad_partial_kernel, size),
        me,
        cot,
        out_weight,
        key_rows,
        value_rows,
        out=[shaped((half, answers, width), bf16)] * 2 + [resident] * 2,
        ins=[SMEM] + [HBM] * 4,
        outs=[VMEM] * 4,
        scratch=[
            pltpu.VMEM((answers, model), bf16),
            pltpu.VMEM((size, model, width), bf16),
            pltpu.SemaphoreType.DMA((3, size)),
            pltpu.SemaphoreType.DMA(()),
        ],
        vmem=49,
    )
    g_other = swap(g_odd, "psg", size, 1)
    block = shaped((answers, width), bf16)
    g_sums = call(add_pair_kernel, g_even, g_other, out=[block] * half, ins=[VMEM] * 2, outs=[VMEM] * half)
    g_parts = [swap(g_sums[d // 2], "psg", size, d) for d in far_first(size)]

    packed = shaped((width + EXTRA, answers), bf16)
    o_even, o_odd = call(
        functools.partial(forward_kernel, size, passages),
        lengths,
        *slots,
        slot_keys,
        slot_values,
        out=[shaped((half, width + EXTRA, answers), bf16)] * 2,
        ins=[SMEM] + [VMEM] * (size + 2),
        outs=[VMEM] * 2,
        scratch=[pltpu.VMEM((size, answers, width), bf16), pltpu.VMEM((key_count, PAIR), f32)],
        vmem=16,
    )

    o_other = swap(o_odd, "psg", size, 1)
    o_pairs = call(merge_pair_kernel, o_even, o_other, out=[packed] * half, ins=[VMEM] * 2, outs=[VMEM] * half)
    arrived = [swap(o_pairs[d // 2], "psg", size, d) for d in far_first(size)]
    context_grad = call(add_all_kernel, g_sums[0], *g_parts, out=block, ins=[VMEM] * half, outs=VMEM)
    cg_even = spread(context_grad, size)
    context = call(
        functools.partial(merge_final_kernel, half),
        o_pairs[0],
        *arrived,
        context_grad,
        out=shaped((answers + 4 * heads, width), bf16),
        ins=[VMEM] * (half + 1),
        outs=VMEM,
    )
    c_even = spread(context, size)
    c_odd = across(c_even, size)
    c_slots = interleaved(c_even, c_odd)
    g_slots = interleaved(cg_even, across(cg_even, size))

    def backward(chosen, carried):
        count = len(chosen)
        pick = slice(chosen[0], chosen[0] + count)
        fixed = 2 + 3 * count + 2
        return call(
            functools.partial(backward_kernel, chosen, len(carried), passages),
            me,
            lengths,
            *slots[pick],
            *g_slots[pick],
            *c_slots[pick],
            slot_keys,
            slot_values,
            *carried,
            out=[shaped((key_count, inner), bf16)] * 2 + [shaped((count // 2, width, answers), bf16)] * 2,
            ins=[SMEM, SMEM] + [VMEM] * (3 * count + 2) + [ANY] * len(carried),
            outs=[ANY, ANY, VMEM, VMEM],
            scratch=[
                pltpu.VMEM((count, answers, width), bf16),
                pltpu.VMEM((count, answers, width), bf16),
                pltpu.VMEM((count, 2 * heads, answers), f32),
            ]
            + [pltpu.VMEM((count, key_count, width), bf16)] * 2
            + [pltpu.VMEM((key_count, PAIR), f32), pltpu.SemaphoreType.DMA((2, count))],
            vmem=16,
            alias={fixed + i: i for i in range(len(carried))},
        )

    def owners_sums(even, odd, count):
        other = swap(odd, "psg", size, 1)
        return call(
            add_pair_kernel,
            even,
            other,
            out=[shaped((width, answers), bf16)] * count,
            ins=[VMEM] * 2,
            outs=[VMEM] * count,
        )

    key_grad, value_grad, far_even, far_odd = backward(range(half, size), ())
    far_sums = owners_sums(far_even, far_odd, half // 2)
    key_grad, value_grad, near_even, near_odd = backward(range(half), (key_grad, value_grad))
    near_sums = owners_sums(near_even, near_odd, half // 2)
    sums = near_sums + far_sums
    dq_parts = [swap(sums[d // 2], "psg", size, d) for d in far_first(size)]
    query_grad = call(add_all_transposed_kernel, sums[0], *dq_parts, out=block, ins=[VMEM] * half, outs=VMEM)

    pack = call(pack_kernel, *c_even, out=shaped((half, answers, width), bf16), ins=[VMEM] * half, outs=VMEM)
    cots = [cot] + [swap(cot, "dp", dp, d) for d in range(1, dp)]
    packs = [pack] + [swap(pack, "dp", dp, d) for d in range(1, dp)]
    packs_odd = [swap(packs[d], "psg", size, 1) for d in range(1, dp)]
    layer_out = call(
        functools.partial(layer_out_kernel, size),
        me,
        *c_slots,
        out_weight,
        out=shaped((answers, model), bf16),
        ins=[SMEM] + [VMEM] * size + [ANY],
        outs=VMEM,
        scratch=[pltpu.VMEM((size, model, width), bf16), pltpu.SemaphoreType.DMA((size,))],
    )
    weight_grad = call(
        functools.partial(weight_grad_kernel, size, dp, answers),
        me,
        *cots,
        *packs,
        *packs_odd,
        *c_odd,
        out=shaped((model, inner), f32),
        ins=[SMEM] + [VMEM] * (3 * dp - 1 + half),
        outs=ANY,
        scratch=[
            pltpu.VMEM((model, dp * answers), bf16),
            pltpu.VMEM((size, model, width), f32),
            pltpu.SemaphoreType.DMA((size,)),
        ],
        vmem=16,
    )
    return (
        layer_out[None],
        weight_grad,
        query_grad[None],
        key_grad.reshape(keys.shape),
        value_grad.reshape(values.shape),
    )


def spread_heads(factor):
    return jnp.transpose(factor, (0, 2, 1))[..., None]


def general_device(queries, keys, values, lengths, out_weight, out_cotangent):
    question_count, passages, passage_len, inner_dim = keys.shape
    key_count = passages * passage_len
    answer_len = queries.shape[1]
    head_split = (question_count, answer_len, inner_dim // HEAD_SIZE, HEAD_SIZE)
    key_split = (question_count, key_count, inner_dim // HEAD_SIZE, HEAD_SIZE)
    einsum = functools.partial(jnp.einsum, preferred_element_type=jnp.float32)
    query_heads = lax.all_gather(queries, "psg", axis=2, tiled=True).reshape(head_split)
    key_heads = keys.reshape(key_split)
    value_heads = values.reshape(key_split)
    positions = jnp.arange(passage_len, dtype=jnp.int32)
    valid = (positions[None, None, :] < lengths[:, :, None]).reshape(question_count, 1, 1, key_count)
    scores = einsum("bihe,bkhe->bhik", query_heads, key_heads)
    row_max = lax.pmax(jnp.max(jnp.where(valid, scores, -jnp.inf), axis=3), "psg")
    weights = jnp.where(valid, jnp.exp(scores - row_max[..., None]), 0.0)
    output = einsum("bhik,bkhe->bihe", weights.astype(jnp.bfloat16), value_heads)
    row_sum, output = lax.psum((jnp.sum(weights, axis=3), output), "psg")
    context = (output / spread_heads(row_sum)).astype(jnp.bfloat16)
    context_rows = context.reshape(question_count * answer_len, inner_dim)
    grad_rows = out_cotangent.reshape(question_count * answer_len, -1)
    layer_out = jnp.dot(context_rows, out_weight.T, preferred_element_type=jnp.float32).astype(jnp.bfloat16)
    weight_grad = lax.psum(
        jnp.dot(grad_rows.T, context_rows, preferred_element_type=jnp.float32).astype(jnp.bfloat16), "dp"
    ).astype(jnp.float32)
    context_grad = lax.psum(jnp.dot(grad_rows, out_weight, preferred_element_type=jnp.float32), "psg").astype(
        jnp.bfloat16
    )
    grad_heads = context_grad.reshape(head_split)
    products = grad_heads.astype(jnp.float32) * context.astype(jnp.float32)
    row_dots = jnp.transpose(jnp.sum(products, axis=3), (0, 2, 1))
    probs = weights / row_sum[..., None]
    prob_grad = einsum("bihe,bkhe->bhik", grad_heads, value_heads)
    score_grad = (probs * (prob_grad - row_dots[..., None])).astype(jnp.bfloat16)
    value_grad = einsum("bhik,bihe->bkhe", probs.astype(jnp.bfloat16), grad_heads)
    key_grad = einsum("bhik,bihe->bkhe", score_grad, query_heads)
    query_terms = einsum("bhik,bkhe->bihe", score_grad, key_heads).reshape(question_count, answer_len, inner_dim)
    query_grad = lax.psum_scatter(query_terms, "psg", scatter_dimension=2, tiled=True)
    return (
        layer_out.reshape(question_count, answer_len, -1),
        weight_grad,
        query_grad.astype(jnp.bfloat16),
        key_grad.astype(jnp.bfloat16).reshape(keys.shape),
        value_grad.astype(jnp.bfloat16).reshape(values.shape),
    )


def solution(mesh):
    dp, size = mesh.shape["dp"], mesh.shape["psg"]

    def per_device(queries, keys, values, lengths, out_weight, out_cotangent):
        return fast_device(dp, size, queries, keys, values, lengths, out_weight, out_cotangent)

    def step(queries, keys, values, lengths, out_weight, out_cotangent):
        width = queries.shape[2] // size
        direct = (
            size in (4, 8)
            and dp in (2, 4)
            and keys.shape[0] == dp
            and width % PAIR == 0
            and 3 * (width // HEAD_SIZE) <= EXTRA
            and 2 * (width // HEAD_SIZE) % 8 == 0
            and queries.shape[1] % 128 == 0
            and keys.shape[2] % 16 == 0
            and (out_weight.shape[0] // size) % width == 0
        )
        body = jax.shard_map(
            per_device if direct else general_device,
            mesh=mesh,
            in_specs=(
                P("dp", None, "psg"),
                P("dp", "psg", None, None),
                P("dp", "psg", None, None),
                P("dp", "psg"),
                P("psg", None),
                P("dp", None, "psg"),
            ),
            out_specs=(
                P("dp", None, "psg"),
                P("psg", None),
                P("dp", None, "psg"),
                P("dp", "psg", None, None),
                P("dp", "psg", None, None),
            ),
            check_vma=False,
        )
        return body(queries, keys, values, lengths, out_weight, out_cotangent)

    return step
```

```python
import functools

import jax
import jax.numpy as jnp
from jax import lax
from jax.experimental import pallas as pl
from jax.experimental.pallas import tpu as pltpu
from jax.sharding import PartitionSpec as P

HEAD_SIZE = 64
PAIR = 2 * HEAD_SIZE
MASKED = -1e30
EXTRA = 16
MIB = 1 << 20

NT = (((1,), (1,)), ((), ()))
NN = (((1,), (0,)), ((), ()))
TN = (((0,), (0,)), ((), ()))
ANY = pl.BlockSpec(memory_space=pl.ANY)
VMEM = pl.BlockSpec(memory_space=pltpu.VMEM)
SMEM = pl.BlockSpec(memory_space=pltpu.SMEM)
HBM = pl.BlockSpec(memory_space=pltpu.HBM)


def dot(a, b, dims):
    return lax.dot_general(a, b, dims, preferred_element_type=jnp.float32)


def swap(x, axis, size, distance):
    return lax.ppermute(x, axis, [(j, j ^ distance) for j in range(size)])


def call(kernel, *args, out, ins, outs, scratch=(), vmem=8, alias=None):
    return pl.pallas_call(
        kernel,
        out_shape=out,
        in_specs=ins,
        out_specs=outs,
        scratch_shapes=list(scratch),
        input_output_aliases=alias or {},
        compiler_params=pltpu.CompilerParams(vmem_limit_bytes=vmem * MIB),
    )(*args)


def far_first(size):
    return range(size - 2, 0, -2)


def spread(x, size):
    even = [x] + [None] * (size // 2 - 1)
    for d in far_first(size):
        even[d // 2] = swap(x, "psg", size, d)
    return even


def across(blocks, size):
    return [swap(b, "psg", size, 1) for b in blocks]


def block_stack(x, lane_low):
    zero = jnp.zeros_like(x)
    return jnp.concatenate([jnp.where(lane_low, x, zero), jnp.where(lane_low, zero, x)], axis=0)


def diagonal(x):
    rows = x.shape[1] // 2
    return jnp.concatenate([x[:HEAD_SIZE, :rows], x[HEAD_SIZE:, rows:]], axis=0)


def mask_bias(lengths_ref, passages, passage_len):
    row = lax.broadcasted_iota(jnp.int32, (passage_len, PAIR), 0)
    return jnp.concatenate([jnp.where(row < lengths_ref[0, p], 0.0, MASKED) for p in range(passages)], axis=0)


def split3(x):
    high = x.astype(jnp.bfloat16).astype(jnp.float32)
    middle = (x - high).astype(jnp.bfloat16).astype(jnp.float32)
    return high, middle, (x - high - middle).astype(jnp.bfloat16).astype(jnp.float32)


def thirds(x):
    pad = jnp.zeros((EXTRA - 3 * x.shape[0], x.shape[1]), jnp.float32)
    return jnp.concatenate([*split3(x), pad], axis=0).astype(jnp.bfloat16)


def unite(rows, heads):
    wide = rows.astype(jnp.float32)
    return wide[:heads] + wide[heads : 2 * heads] + wide[2 * heads : 3 * heads]


def columns_of(ref, me, slot, width):
    owner = jnp.bitwise_xor(me, slot)
    return ref.at[:, pl.ds(pl.multiple_of(owner * width, width), width)]


def forward_kernel(size, passages, lengths_ref, *refs):
    q_refs = refs[:size]
    keys_ref, values_ref, even_ref, odd_ref, weights_ref, tops_ref, q_buf, s_buf, bias_ref = refs[size:]
    width = q_buf.shape[2]
    pairs = width // PAIR
    for s in range(size):
        q_buf[s] = q_refs[s][...]
    bias_ref[...] = mask_bias(lengths_ref, passages, keys_ref.shape[1] // passages)
    lane_low = lax.broadcasted_iota(jnp.int32, (1, PAIR), 1) < HEAD_SIZE

    def score(s, p):
        lanes = slice(p * PAIR, (p + 1) * PAIR)
        queries = block_stack(q_buf[s, :, lanes], lane_low)
        bias = bias_ref[...]
        scores = dot(keys_ref[s, :, lanes], queries, NT) + jnp.concatenate([bias, bias], axis=1)
        s_buf[p] = scores
        return jnp.max(scores, axis=0, keepdims=True)

    def mix(s, p, top, out_ref, k):
        lanes = slice(p * PAIR, (p + 1) * PAIR)
        weights = jnp.exp(s_buf[p] - top)
        total = jnp.sum(weights, axis=0, keepdims=True)
        rounded = weights.astype(jnp.bfloat16)
        weights_ref[s * pairs + p] = rounded
        mixed = dot(values_ref[s, :, lanes], rounded, TN) / total
        out_ref[k, lanes, :] = diagonal(mixed).astype(jnp.bfloat16)
        return top + jnp.log(total)

    def one_slot(s, out_ref, k, first_top):
        tops, lses = [first_top], []
        for p in range(pairs):
            if p + 1 < pairs:
                tops.append(score(s, p + 1))
            else:
                following = score(jnp.minimum(s + 1, size - 1), 0) if pairs > 1 else None
            lses.append(mix(s, p, tops[p], out_ref, k))
        if following is None:
            following = score(jnp.minimum(s + 1, size - 1), 0)
        n = first_top.shape[1] // 2
        tops_ref[s] = jnp.concatenate([x[:, h * n : (h + 1) * n] for x in tops for h in range(2)], axis=0)
        rows = jnp.concatenate([x[:, h * n : (h + 1) * n] for x in lses for h in range(2)], axis=0)
        out_ref[k, width:, :] = thirds(rows)
        return following

    def body(k, top):
        top = one_slot(2 * k, even_ref, k, top)
        return one_slot(2 * k + 1, odd_ref, k, top)

    lax.fori_loop(0, size // 2, body, score(0, 0))


def merge(blocks):
    width = blocks[0].shape[0] - EXTRA
    heads = width // HEAD_SIZE
    lses = [unite(b[width:], heads) for b in blocks]
    top = functools.reduce(jnp.maximum, lses)
    shares = [jnp.exp(x - top) for x in lses]
    total = sum(shares)
    shares = [x / total for x in shares]
    outs = []
    for h in range(heads):
        rows = slice(h * HEAD_SIZE, (h + 1) * HEAD_SIZE)
        outs.append(sum(x[h : h + 1] * b[rows].astype(jnp.float32) for b, x in zip(blocks, shares)))
    return jnp.concatenate(outs, axis=0), top + jnp.log(total)


def merge_pair_kernel(a_ref, b_ref, *out_refs):
    for k, out_ref in enumerate(out_refs):
        out, lse = merge([a_ref[k], b_ref[k]])
        width = out.shape[0]
        out_ref[:width, :] = out.astype(jnp.bfloat16)
        out_ref[width:, :] = thirds(lse)


def merge_final_kernel(count, *refs):
    grad_ref, out_ref = refs[count:]
    out, lse = merge([r[...] for r in refs[:count]])
    context = out.T.astype(jnp.bfloat16)
    answers, _ = context.shape
    out_ref[:answers, :] = context
    product = (context.astype(jnp.float32) * grad_ref[...].astype(jnp.float32)).T
    dots = [
        jnp.sum(product[h * HEAD_SIZE : (h + 1) * HEAD_SIZE], axis=0, keepdims=True) for h in range(lse.shape[0])
    ]
    high, middle, low = split3(jnp.concatenate([lse] + dots, axis=0))
    top = jnp.concatenate([high, middle], axis=1)
    bottom = jnp.concatenate([low, jnp.zeros_like(low)], axis=1)
    out_ref[answers:, :] = jnp.concatenate([top, bottom], axis=0).astype(jnp.bfloat16)


def stats_of(block_ref, answers):
    rows = block_ref[answers:, :].astype(jnp.float32)
    n = rows.shape[0] // 2
    return rows[:n, :answers] + rows[:n, answers:] + rows[n:, :answers]


def backward_kernel(slots, carried, me_ref, *refs):
    count = len(slots)
    q_refs, g_refs, c_refs = refs[:count], refs[count : 2 * count], refs[2 * count : 3 * count]
    keys_ref, values_ref, weights_ref, tops_ref = refs[3 * count : 3 * count + 4]
    dk_ref, dv_ref, even_ref, odd_ref, q_buf, g_buf, st_buf, p_buf, dk_buf, dv_buf, sem = refs[3 * count + 4 + carried :]
    me = me_ref[0]
    answers, width = q_buf.shape[1:]
    pairs = width // PAIR
    first = slots[0]
    heads = width // HEAD_SIZE

    def dk_copy(i):
        return pltpu.make_async_copy(dk_buf.at[i], columns_of(dk_ref, me, first + i, width), sem.at[0, i])

    def dv_copy(i):
        return pltpu.make_async_copy(dv_buf.at[i], columns_of(dv_ref, me, first + i, width), sem.at[1, i])

    lane_low = lax.broadcasted_iota(jnp.int32, (1, PAIR), 1) < HEAD_SIZE
    for i in range(count):
        stats = stats_of(c_refs[i], answers)
        share = jnp.exp(tops_ref[first + i] - stats[:heads])
        st_buf[i] = jnp.concatenate([share, stats[heads:]], axis=0)
        q_buf[i] = q_refs[i][...]
        g_buf[i] = g_refs[i][...]

    def grads_of(i, p):
        return block_stack(g_buf[i, :, p * PAIR : (p + 1) * PAIR], lane_low)

    def prob_grad(i, p):
        p_buf[p] = dot(values_ref[first + i, :, p * PAIR : (p + 1) * PAIR], grads_of(i, p), NT)

    def row_pair(rows, at):
        return jnp.concatenate([rows[at : at + 1], rows[at + 1 : at + 2]], axis=1)

    def rest(i, p, out_ref, k):
        lanes = slice(p * PAIR, (p + 1) * PAIR)
        queries = block_stack(q_buf[i, :, lanes], lane_low)
        stats = st_buf[i]
        probs = weights_ref[(first + i) * pairs + p].astype(jnp.float32) * row_pair(stats, 2 * p)
        score_grad = (probs * (p_buf[p] - row_pair(stats, heads + 2 * p))).astype(jnp.bfloat16)
        dv_buf[i, :, lanes] = dot(probs.astype(jnp.bfloat16), grads_of(i, p), NN).astype(jnp.bfloat16)
        dk_buf[i, :, lanes] = dot(score_grad, queries, NN).astype(jnp.bfloat16)
        out_ref[k, lanes, :] = diagonal(dot(keys_ref[first + i, :, lanes], score_grad, TN)).astype(jnp.bfloat16)

    def one_slot(i, out_ref, k):
        for p in range(pairs):
            if p + 1 < pairs:
                prob_grad(i, p + 1)
                rest(i, p, out_ref, k)
            else:
                rest(i, p, out_ref, k) if pairs == 1 else None
                prob_grad(jnp.minimum(i + 1, count - 1), 0)
                rest(i, p, out_ref, k) if pairs > 1 else None
        dk_copy(i).start()
        dv_copy(i).start()

    def body(k, carry):
        one_slot(2 * k, even_ref, k)
        one_slot(2 * k + 1, odd_ref, k)
        return carry

    prob_grad(0, 0)
    lax.fori_loop(0, count // 2, body, 0)
    for i in range(count):
        dk_copy(i).wait()
        dv_copy(i).wait()


def add_pair_kernel(a_ref, b_ref, *out_refs):
    for k, out_ref in enumerate(out_refs):
        out_ref[...] = (a_ref[k].astype(jnp.float32) + b_ref[k].astype(jnp.float32)).astype(jnp.bfloat16)


def add_all_kernel(*refs):
    total = refs[0][...].astype(jnp.float32)
    for r in refs[1:-1]:
        total += r[...].astype(jnp.float32)
    refs[-1][...] = total.astype(jnp.bfloat16)


def add_all_transposed_kernel(*refs):
    total = refs[0][...].astype(jnp.float32)
    for r in refs[1:-1]:
        total += r[...].astype(jnp.float32)
    refs[-1][...] = total.T.astype(jnp.bfloat16)


def grad_partial_kernel(size, me_ref, cot_ref, weight_ref, keys_ref, values_ref, *refs):
    even_ref, odd_ref, k_out, v_out, cot_buf, w_buf, sem, cot_sem = refs
    me = me_ref[0]
    width = w_buf.shape[2]

    def copy(ref, buf, lane, s):
        return pltpu.make_async_copy(columns_of(ref, me, s, width), buf.at[s], sem.at[lane, s])

    order = list(range(1, size, 2)) + list(range(0, size, 2))
    cot_copy = pltpu.make_async_copy(cot_ref, cot_buf, cot_sem)
    cot_copy.start()
    for s in order:
        copy(weight_ref, w_buf, 0, s).start()
    for s in range(size):
        copy(keys_ref, k_out, 1, s).start()
        copy(values_ref, v_out, 2, s).start()
    cot_copy.wait()
    cot = cot_buf[...]
    for s in order:
        copy(weight_ref, w_buf, 0, s).wait()
        (odd_ref if s % 2 else even_ref)[s // 2] = dot(cot, w_buf[s], NN).astype(jnp.bfloat16)
    for s in range(size):
        copy(keys_ref, k_out, 1, s).wait()
        copy(values_ref, v_out, 2, s).wait()


def layer_out_kernel(size, me_ref, *refs):
    weight_ref, out_ref = refs[size:]
    me = me_ref[0]
    answers, width = out_ref.shape[0], refs[0].shape[1]
    total = None
    for s in range(size):
        part = dot(refs[s][:answers, :], columns_of(weight_ref, me, s, width)[...], NT)
        total = part if total is None else total + part
    out_ref[...] = total.astype(jnp.bfloat16)


def weight_grad_kernel(size, groups, answers, me_ref, *refs):
    half = size // 2
    cots, refs = refs[:groups], refs[groups:]
    packs, packs_odd, own = refs[:groups], refs[groups : 2 * groups - 1], refs[2 * groups - 1 : 2 * groups - 1 + half]
    out_ref, cot_buf, out_buf, sem = refs[2 * groups - 1 + half :]
    me = me_ref[0]
    width = out_buf.shape[2]
    for g in range(groups):
        cot_buf[:, g * answers : (g + 1) * answers] = cots[g][...].T

    def out_copy(s):
        return pltpu.make_async_copy(out_buf.at[s], columns_of(out_ref, me, s, width), sem.at[s])

    for s in range(size):
        k = s // 2
        if s % 2:
            blocks = [own[k][:answers, :]] + [o[k] for o in packs_odd]
        else:
            blocks = [o[k] for o in packs]
        out_buf[s] = dot(cot_buf[...], jnp.concatenate(blocks, axis=0), NN)
        out_copy(s).start()
    for s in range(size):
        out_copy(s).wait()


def pack_kernel(*refs):
    out_ref = refs[-1]
    for k in range(out_ref.shape[0]):
        out_ref[k] = refs[k][: out_ref.shape[1], :]


def shaped(shape, dtype):
    return jax.ShapeDtypeStruct(shape, dtype)


def fast_device(dp, size, queries, keys, values, lengths, out_weight, out_cotangent):
    bf16, f32 = jnp.bfloat16, jnp.float32
    passages, passage_len, inner = keys.shape[1:]
    key_count = passages * passage_len
    answers, width = queries.shape[1:]
    half = size // 2
    heads = width // HEAD_SIZE
    model = out_weight.shape[0]
    me = lax.axis_index("psg").reshape(1)
    query = queries[0]
    cot = out_cotangent[0]
    key_rows = keys.reshape(key_count, inner)
    value_rows = values.reshape(key_count, inner)

    def interleaved(even, odd):
        return [r for pair in zip(even, odd) for r in pair]

    q_even = spread(query, size)
    slots = interleaved(q_even, across(q_even, size))

    resident = shaped((size, key_count, width), bf16)
    g_even, g_odd, slot_keys, slot_values = call(
        functools.partial(grad_partial_kernel, size),
        me,
        cot,
        out_weight,
        key_rows,
        value_rows,
        out=[shaped((half, answers, width), bf16)] * 2 + [resident] * 2,
        ins=[SMEM] + [HBM] * 4,
        outs=[VMEM] * 4,
        scratch=[
            pltpu.VMEM((answers, model), bf16),
            pltpu.VMEM((size, model, width), bf16),
            pltpu.SemaphoreType.DMA((3, size)),
            pltpu.SemaphoreType.DMA(()),
        ],
        vmem=49,
    )
    g_other = swap(g_odd, "psg", size, 1)
    block = shaped((answers, width), bf16)
    g_sums = call(add_pair_kernel, g_even, g_other, out=[block] * half, ins=[VMEM] * 2, outs=[VMEM] * half)
    g_parts = [swap(g_sums[d // 2], "psg", size, d) for d in far_first(size)]

    packed = shaped((width + EXTRA, answers), bf16)
    pairs = width // PAIR
    o_even, o_odd, weights, tops = call(
        functools.partial(forward_kernel, size, passages),
        lengths,
        *slots,
        slot_keys,
        slot_values,
        out=[shaped((half, width + EXTRA, answers), bf16)] * 2
        + [shaped((size * pairs, key_count, 2 * answers), bf16), shaped((size, heads, answers), f32)],
        ins=[SMEM] + [VMEM] * (size + 2),
        outs=[VMEM] * 4,
        scratch=[
            pltpu.VMEM((size, answers, width), bf16),
            pltpu.VMEM((pairs, key_count, 2 * answers), f32),
            pltpu.VMEM((key_count, PAIR), f32),
        ],
        vmem=16,
    )

    o_other = swap(o_odd, "psg", size, 1)
    o_pairs = call(merge_pair_kernel, o_even, o_other, out=[packed] * half, ins=[VMEM] * 2, outs=[VMEM] * half)
    arrived = [swap(o_pairs[d // 2], "psg", size, d) for d in far_first(size)]
    context_grad = call(add_all_kernel, g_sums[0], *g_parts, out=block, ins=[VMEM] * half, outs=VMEM)
    cg_even = spread(context_grad, size)
    context = call(
        functools.partial(merge_final_kernel, half),
        o_pairs[0],
        *arrived,
        context_grad,
        out=shaped((answers + 4 * heads, width), bf16),
        ins=[VMEM] * (half + 1),
        outs=VMEM,
    )
    c_even = spread(context, size)
    c_odd = across(c_even, size)
    c_slots = interleaved(c_even, c_odd)
    g_slots = interleaved(cg_even, across(cg_even, size))

    def backward(chosen, carried):
        count = len(chosen)
        pick = slice(chosen[0], chosen[0] + count)
        fixed = 1 + 3 * count + 4
        return call(
            functools.partial(backward_kernel, chosen, len(carried)),
            me,
            *slots[pick],
            *g_slots[pick],
            *c_slots[pick],
            slot_keys,
            slot_values,
            weights,
            tops,
            *carried,
            out=[shaped((key_count, inner), bf16)] * 2 + [shaped((count // 2, width, answers), bf16)] * 2,
            ins=[SMEM] + [VMEM] * (3 * count + 4) + [ANY] * len(carried),
            outs=[ANY, ANY, VMEM, VMEM],
            scratch=[
                pltpu.VMEM((count, answers, width), bf16),
                pltpu.VMEM((count, answers, width), bf16),
                pltpu.VMEM((count, 2 * heads, answers), f32),
            ]
            + [pltpu.VMEM((pairs, key_count, 2 * answers), f32)]
            + [pltpu.VMEM((count, key_count, width), bf16)] * 2
            + [pltpu.SemaphoreType.DMA((2, count))],
            vmem=16,
            alias={fixed + i: i for i in range(len(carried))},
        )

    def owners_sums(even, odd, count):
        other = swap(odd, "psg", size, 1)
        return call(
            add_pair_kernel,
            even,
            other,
            out=[shaped((width, answers), bf16)] * count,
            ins=[VMEM] * 2,
            outs=[VMEM] * count,
        )

    key_grad, value_grad, far_even, far_odd = backward(range(half, size), ())
    far_sums = owners_sums(far_even, far_odd, half // 2)
    key_grad, value_grad, near_even, near_odd = backward(range(half), (key_grad, value_grad))
    near_sums = owners_sums(near_even, near_odd, half // 2)
    sums = near_sums + far_sums
    dq_parts = [swap(sums[d // 2], "psg", size, d) for d in far_first(size)]
    query_grad = call(add_all_transposed_kernel, sums[0], *dq_parts, out=block, ins=[VMEM] * half, outs=VMEM)

    pack = call(pack_kernel, *c_even, out=shaped((half, answers, width), bf16), ins=[VMEM] * half, outs=VMEM)
    cots = [cot] + [swap(cot, "dp", dp, d) for d in range(1, dp)]
    packs = [pack] + [swap(pack, "dp", dp, d) for d in range(1, dp)]
    packs_odd = [swap(packs[d], "psg", size, 1) for d in range(1, dp)]
    layer_out = call(
        functools.partial(layer_out_kernel, size),
        me,
        *c_slots,
        out_weight,
        out=shaped((answers, model), bf16),
        ins=[SMEM] + [VMEM] * (size + 1),
        outs=VMEM,
    )
    weight_grad = call(
        functools.partial(weight_grad_kernel, size, dp, answers),
        me,
        *cots,
        *packs,
        *packs_odd,
        *c_odd,
        out=shaped((model, inner), f32),
        ins=[SMEM] + [VMEM] * (3 * dp - 1 + half),
        outs=ANY,
        scratch=[
            pltpu.VMEM((model, dp * answers), bf16),
            pltpu.VMEM((size, model, width), f32),
            pltpu.SemaphoreType.DMA((size,)),
        ],
        vmem=16,
    )
    return (
        layer_out[None],
        weight_grad,
        query_grad[None],
        key_grad.reshape(keys.shape),
        value_grad.reshape(values.shape),
    )


def spread_heads(factor):
    return jnp.transpose(factor, (0, 2, 1))[..., None]


def general_device(queries, keys, values, lengths, out_weight, out_cotangent):
    question_count, passages, passage_len, inner_dim = keys.shape
    key_count = passages * passage_len
    answer_len = queries.shape[1]
    head_split = (question_count, answer_len, inner_dim // HEAD_SIZE, HEAD_SIZE)
    key_split = (question_count, key_count, inner_dim // HEAD_SIZE, HEAD_SIZE)
    einsum = functools.partial(jnp.einsum, preferred_element_type=jnp.float32)
    query_heads = lax.all_gather(queries, "psg", axis=2, tiled=True).reshape(head_split)
    key_heads = keys.reshape(key_split)
    value_heads = values.reshape(key_split)
    positions = jnp.arange(passage_len, dtype=jnp.int32)
    valid = (positions[None, None, :] < lengths[:, :, None]).reshape(question_count, 1, 1, key_count)
    scores = einsum("bihe,bkhe->bhik", query_heads, key_heads)
    row_max = lax.pmax(jnp.max(jnp.where(valid, scores, -jnp.inf), axis=3), "psg")
    weights = jnp.where(valid, jnp.exp(scores - row_max[..., None]), 0.0)
    output = einsum("bhik,bkhe->bihe", weights.astype(jnp.bfloat16), value_heads)
    row_sum, output = lax.psum((jnp.sum(weights, axis=3), output), "psg")
    context = (output / spread_heads(row_sum)).astype(jnp.bfloat16)
    context_rows = context.reshape(question_count * answer_len, inner_dim)
    grad_rows = out_cotangent.reshape(question_count * answer_len, -1)
    layer_out = jnp.dot(context_rows, out_weight.T, preferred_element_type=jnp.float32).astype(jnp.bfloat16)
    weight_grad = lax.psum(
        jnp.dot(grad_rows.T, context_rows, preferred_element_type=jnp.float32).astype(jnp.bfloat16), "dp"
    ).astype(jnp.float32)
    context_grad = lax.psum(jnp.dot(grad_rows, out_weight, preferred_element_type=jnp.float32), "psg").astype(
        jnp.bfloat16
    )
    grad_heads = context_grad.reshape(head_split)
    products = grad_heads.astype(jnp.float32) * context.astype(jnp.float32)
    row_dots = jnp.transpose(jnp.sum(products, axis=3), (0, 2, 1))
    probs = weights / row_sum[..., None]
    prob_grad = einsum("bihe,bkhe->bhik", grad_heads, value_heads)
    score_grad = (probs * (prob_grad - row_dots[..., None])).astype(jnp.bfloat16)
    value_grad = einsum("bhik,bihe->bkhe", probs.astype(jnp.bfloat16), grad_heads)
    key_grad = einsum("bhik,bihe->bkhe", score_grad, query_heads)
    query_terms = einsum("bhik,bkhe->bihe", score_grad, key_heads).reshape(question_count, answer_len, inner_dim)
    query_grad = lax.psum_scatter(query_terms, "psg", scatter_dimension=2, tiled=True)
    return (
        layer_out.reshape(question_count, answer_len, -1),
        weight_grad,
        query_grad.astype(jnp.bfloat16),
        key_grad.astype(jnp.bfloat16).reshape(keys.shape),
        value_grad.astype(jnp.bfloat16).reshape(values.shape),
    )


def solution(mesh):
    dp, size = mesh.shape["dp"], mesh.shape["psg"]

    def per_device(queries, keys, values, lengths, out_weight, out_cotangent):
        return fast_device(dp, size, queries, keys, values, lengths, out_weight, out_cotangent)

    def step(queries, keys, values, lengths, out_weight, out_cotangent):
        width = queries.shape[2] // size
        direct = (
            size in (4, 8)
            and dp in (2, 4)
            and keys.shape[0] == dp
            and width % PAIR == 0
            and 3 * (width // HEAD_SIZE) <= EXTRA
            and 2 * (width // HEAD_SIZE) % 8 == 0
            and queries.shape[1] % 128 == 0
            and keys.shape[2] % 16 == 0
            and (out_weight.shape[0] // size) % width == 0
        )
        body = jax.shard_map(
            per_device if direct else general_device,
            mesh=mesh,
            in_specs=(
                P("dp", None, "psg"),
                P("dp", "psg", None, None),
                P("dp", "psg", None, None),
                P("dp", "psg"),
                P("psg", None),
                P("dp", None, "psg"),
            ),
            out_specs=(
                P("dp", None, "psg"),
                P("psg", None),
                P("dp", None, "psg"),
                P("dp", "psg", None, None),
                P("dp", "psg", None, None),
            ),
            check_vma=False,
        )
        return body(queries, keys, values, lengths, out_weight, out_cotangent)

    return step
```

```python
import functools

import jax
import jax.numpy as jnp
from jax import lax
from jax.experimental import pallas as pl
from jax.experimental.pallas import tpu as pltpu
from jax.sharding import PartitionSpec as P

HEAD_SIZE = 64
PAIR = 2 * HEAD_SIZE
MASKED = -1e30
EXTRA = 16
MIB = 1 << 20
GRAD_VMEM = 55
ADD_COST = 20

NT = (((1,), (1,)), ((), ()))
NN = (((1,), (0,)), ((), ()))
TN = (((0,), (0,)), ((), ()))
ANY = pl.BlockSpec(memory_space=pl.ANY)
VMEM = pl.BlockSpec(memory_space=pltpu.VMEM)
SMEM = pl.BlockSpec(memory_space=pltpu.SMEM)
HBM = pl.BlockSpec(memory_space=pltpu.HBM)


def dot(a, b, dims):
    return lax.dot_general(a, b, dims, preferred_element_type=jnp.float32)


def swap(x, axis, size, distance):
    return lax.ppermute(x, axis, [(j, j ^ distance) for j in range(size)])


def call(kernel, *args, out, ins, outs, scratch=(), vmem=8, alias=None, cost=None):
    return pl.pallas_call(
        kernel,
        out_shape=out,
        in_specs=ins,
        out_specs=outs,
        scratch_shapes=list(scratch),
        input_output_aliases=alias or {},
        compiler_params=pltpu.CompilerParams(vmem_limit_bytes=int(vmem * MIB)),
        cost_estimate=cost,
    )(*args)


def far_first(size):
    return range(size - 2, 0, -2)


def spread(x, size):
    even = [x] + [None] * (size // 2 - 1)
    for d in far_first(size):
        even[d // 2] = swap(x, "psg", size, d)
    return even


def across(blocks, size):
    return [swap(b, "psg", size, 1) for b in blocks]


def block_stack(x, lane_low):
    zero = jnp.zeros_like(x)
    return jnp.concatenate([jnp.where(lane_low, x, zero), jnp.where(lane_low, zero, x)], axis=0)


def diagonal(x):
    rows = x.shape[1] // 2
    return jnp.concatenate([x[:HEAD_SIZE, :rows], x[HEAD_SIZE:, rows:]], axis=0)


def mask_bias(lengths_ref, passages, passage_len):
    row = lax.broadcasted_iota(jnp.int32, (passage_len, PAIR), 0)
    return jnp.concatenate([jnp.where(row < lengths_ref[0, p], 0.0, MASKED) for p in range(passages)], axis=0)


def split3(x):
    high = x.astype(jnp.bfloat16).astype(jnp.float32)
    middle = (x - high).astype(jnp.bfloat16).astype(jnp.float32)
    return high, middle, (x - high - middle).astype(jnp.bfloat16).astype(jnp.float32)


def thirds(x):
    pad = jnp.zeros((EXTRA - 3 * x.shape[0], x.shape[1]), jnp.float32)
    return jnp.concatenate([*split3(x), pad], axis=0).astype(jnp.bfloat16)


def unite(rows, heads):
    wide = rows.astype(jnp.float32)
    return wide[:heads] + wide[heads : 2 * heads] + wide[2 * heads : 3 * heads]


def columns_of(ref, me, slot, width):
    owner = jnp.bitwise_xor(me, slot)
    return ref.at[:, pl.ds(pl.multiple_of(owner * width, width), width)]


def pair_of(ref, me, slot, width, pair):
    at = jnp.bitwise_xor(me, slot) * width + pair * PAIR
    return ref.at[:, pl.ds(pl.multiple_of(at, PAIR), PAIR)]


def forward_kernel(parity, passages, me_ref, lengths_ref, *refs):
    out_ref, weights_ref, tops_ref, q_buf, s_buf, bias_ref = refs[-6:]
    keys_ref, values_ref = refs[-8:-6]
    me = me_ref[0]
    count, _, width = q_buf.shape
    pairs = width // PAIR
    for k in range(count):
        q_buf[k] = refs[k][...]
    bias_ref[...] = mask_bias(lengths_ref, passages, keys_ref.shape[0] // passages)
    lane_low = lax.broadcasted_iota(jnp.int32, (1, PAIR), 1) < HEAD_SIZE

    def score(k, p):
        queries = block_stack(q_buf[k, :, p * PAIR : (p + 1) * PAIR], lane_low)
        bias = bias_ref[...]
        keys = pair_of(keys_ref, me, 2 * k + parity, width, p)[...]
        scores = dot(keys, queries, NT) + jnp.concatenate([bias, bias], axis=1)
        s_buf[p] = scores
        return jnp.max(scores, axis=0, keepdims=True)

    def mix(k, p, top):
        weights = jnp.exp(s_buf[p] - top)
        total = jnp.sum(weights, axis=0, keepdims=True)
        rounded = weights.astype(jnp.bfloat16)
        weights_ref[k * pairs + p] = rounded
        values = pair_of(values_ref, me, 2 * k + parity, width, p)[...]
        mixed = dot(values, rounded, TN) / total
        out_ref[k, p * PAIR : (p + 1) * PAIR, :] = diagonal(mixed).astype(jnp.bfloat16)
        return top + jnp.log(total)

    def by_head(rows):
        n = rows[0].shape[1] // 2
        return jnp.concatenate([x[:, h * n : (h + 1) * n] for x in rows for h in range(2)], axis=0)

    def one_slot(k, top):
        tops, lses = [top], []
        for p in range(pairs):
            if p + 1 < pairs:
                tops.append(score(k, p + 1))
            elif pairs > 1:
                top = score(jnp.minimum(k + 1, count - 1), 0)
            lses.append(mix(k, p, tops[p]))
        if pairs == 1:
            top = score(jnp.minimum(k + 1, count - 1), 0)
        tops_ref[k] = by_head(tops)
        out_ref[k, width:, :] = thirds(by_head(lses))
        return top

    lax.fori_loop(0, count // 2, lambda k, top: one_slot(2 * k + 1, one_slot(2 * k, top)), score(0, 0))


def merge(blocks):
    width = blocks[0].shape[0] - EXTRA
    heads = width // HEAD_SIZE
    lses = [unite(b[width:], heads) for b in blocks]
    top = functools.reduce(jnp.maximum, lses)
    shares = [jnp.exp(x - top) for x in lses]
    total = sum(shares)
    shares = [x / total for x in shares]
    outs = []
    for h in range(heads):
        rows = slice(h * HEAD_SIZE, (h + 1) * HEAD_SIZE)
        outs.append(sum(x[h : h + 1] * b[rows].astype(jnp.float32) for b, x in zip(blocks, shares)))
    return jnp.concatenate(outs, axis=0), top + jnp.log(total)


def merge_pair_kernel(a_ref, b_ref, *out_refs):
    for k, out_ref in enumerate(out_refs):
        out, lse = merge([a_ref[k], b_ref[k]])
        width = out.shape[0]
        out_ref[:width, :] = out.astype(jnp.bfloat16)
        out_ref[width:, :] = thirds(lse)


def merge_final_kernel(count, *refs):
    grad_ref, out_ref = refs[count:]
    out, lse = merge([r[...] for r in refs[:count]])
    context = out.T.astype(jnp.bfloat16)
    answers, _ = context.shape
    out_ref[:answers, :] = context
    product = (context.astype(jnp.float32) * grad_ref[...].astype(jnp.float32)).T
    dots = [
        jnp.sum(product[h * HEAD_SIZE : (h + 1) * HEAD_SIZE], axis=0, keepdims=True) for h in range(lse.shape[0])
    ]
    high, middle, low = split3(jnp.concatenate([lse] + dots, axis=0))
    top = jnp.concatenate([high, middle], axis=1)
    bottom = jnp.concatenate([low, jnp.zeros_like(low)], axis=1)
    out_ref[answers:, :] = jnp.concatenate([top, bottom], axis=0).astype(jnp.bfloat16)


def stats_of(block_ref, answers):
    rows = block_ref[answers:, :].astype(jnp.float32)
    n = rows.shape[0] // 2
    return rows[:n, :answers] + rows[:n, answers:] + rows[n:, :answers]


def backward_kernel(slots, carried, me_ref, *refs):
    count = len(slots)
    q_refs, g_refs, c_refs = refs[:count], refs[count : 2 * count], refs[2 * count : 3 * count]
    keys_ref, values_ref, *kept = refs[3 * count : 3 * count + 6]
    weights_refs, tops_refs = kept[:2], kept[2:]
    dk_ref, dv_ref, even_ref, odd_ref, q_buf, g_buf, st_buf, p_buf, dk_buf, dv_buf, sem = refs[3 * count + 6 + carried :]
    me = me_ref[0]
    answers, width = q_buf.shape[1:]
    pairs = width // PAIR
    first = slots[0]
    heads = width // HEAD_SIZE

    def dk_copy(i):
        return pltpu.make_async_copy(dk_buf.at[i], columns_of(dk_ref, me, first + i, width), sem.at[0, i])

    def dv_copy(i):
        return pltpu.make_async_copy(dv_buf.at[i], columns_of(dv_ref, me, first + i, width), sem.at[1, i])

    lane_low = lax.broadcasted_iota(jnp.int32, (1, PAIR), 1) < HEAD_SIZE
    for i in range(count):
        stats = stats_of(c_refs[i], answers)
        share = jnp.exp(tops_refs[i % 2][first // 2 + i // 2] - stats[:heads])
        st_buf[i] = jnp.concatenate([share, stats[heads:]], axis=0)
        q_buf[i] = q_refs[i][...]
        g_buf[i] = g_refs[i][...]

    def grads_of(i, p):
        return block_stack(g_buf[i, :, p * PAIR : (p + 1) * PAIR], lane_low)

    def prob_grad(i, p):
        p_buf[p] = dot(pair_of(values_ref, me, first + i, width, p)[...], grads_of(i, p), NT)

    def row_pair(rows, at):
        return jnp.concatenate([rows[at : at + 1], rows[at + 1 : at + 2]], axis=1)

    def rest(i, p, parity, k):
        out_ref = (even_ref, odd_ref)[parity]
        lanes = slice(p * PAIR, (p + 1) * PAIR)
        queries = block_stack(q_buf[i, :, lanes], lane_low)
        stats = st_buf[i]
        probs = weights_refs[parity][(first // 2 + k) * pairs + p].astype(jnp.float32) * row_pair(stats, 2 * p)
        score_grad = (probs * (p_buf[p] - row_pair(stats, heads + 2 * p))).astype(jnp.bfloat16)
        dv_buf[i, :, lanes] = dot(probs.astype(jnp.bfloat16), grads_of(i, p), NN).astype(jnp.bfloat16)
        dk_buf[i, :, lanes] = dot(score_grad, queries, NN).astype(jnp.bfloat16)
        out_ref[k, lanes, :] = diagonal(dot(pair_of(keys_ref, me, first + i, width, p)[...], score_grad, TN)).astype(
            jnp.bfloat16
        )

    def one_slot(i, parity, k):
        for p in range(pairs):
            if p + 1 < pairs:
                prob_grad(i, p + 1)
                rest(i, p, parity, k)
            else:
                rest(i, p, parity, k) if pairs == 1 else None
                prob_grad(jnp.minimum(i + 1, count - 1), 0)
                rest(i, p, parity, k) if pairs > 1 else None
        dk_copy(i).start()
        dv_copy(i).start()

    def body(k, carry):
        one_slot(2 * k, 0, k)
        one_slot(2 * k + 1, 1, k)
        return carry

    prob_grad(0, 0)
    lax.fori_loop(0, count // 2, body, 0)
    for i in range(count):
        dk_copy(i).wait()
        dv_copy(i).wait()


def add_pair_kernel(a_ref, b_ref, *out_refs):
    for k, out_ref in enumerate(out_refs):
        out_ref[...] = (a_ref[k].astype(jnp.float32) + b_ref[k].astype(jnp.float32)).astype(jnp.bfloat16)


def add_all_kernel(*refs):
    total = refs[0][...].astype(jnp.float32)
    for r in refs[1:-1]:
        total += r[...].astype(jnp.float32)
    refs[-1][...] = total.astype(jnp.bfloat16)


def add_all_transposed_kernel(*refs):
    total = refs[0][...].astype(jnp.float32)
    for r in refs[1:-1]:
        total += r[...].astype(jnp.float32)
    refs[-1][...] = total.T.astype(jnp.bfloat16)


def grad_partial_kernel(size, me_ref, cot_ref, weight_ref, even_ref, odd_ref, cot_buf, w_buf, sem, cot_sem):
    me = me_ref[0]
    width = w_buf.shape[2]

    def copy(s):
        return pltpu.make_async_copy(columns_of(weight_ref, me, s, width), w_buf.at[s], sem.at[s])

    cot_copy = pltpu.make_async_copy(cot_ref, cot_buf, cot_sem)
    cot_copy.start()
    order = list(range(1, size, 2)) + list(range(0, size, 2))
    for s in order:
        copy(s).start()
    cot_copy.wait()
    cot = cot_buf[...]
    for s in order:
        copy(s).wait()
        (odd_ref if s % 2 else even_ref)[s // 2] = dot(cot, w_buf[s], NN).astype(jnp.bfloat16)


def layer_out_kernel(size, me_ref, *refs):
    weight_ref, out_ref = refs[size:]
    me = me_ref[0]
    answers, width = out_ref.shape[0], refs[0].shape[1]
    total = None
    for s in range(size):
        part = dot(refs[s][:answers, :], columns_of(weight_ref, me, s, width)[...], NT)
        total = part if total is None else total + part
    out_ref[...] = total.astype(jnp.bfloat16)


def weight_grad_kernel(size, groups, answers, me_ref, *refs):
    half = size // 2
    cots, refs = refs[:groups], refs[groups:]
    packs, packs_odd, own = refs[:groups], refs[groups : 2 * groups - 1], refs[2 * groups - 1 : 2 * groups - 1 + half]
    out_ref, cot_buf, out_buf, sem = refs[2 * groups - 1 + half :]
    me = me_ref[0]
    width = out_buf.shape[2]
    for g in range(groups):
        cot_buf[:, g * answers : (g + 1) * answers] = cots[g][...].T

    def out_copy(s):
        return pltpu.make_async_copy(out_buf.at[s], columns_of(out_ref, me, s, width), sem.at[s])

    for s in range(size):
        k = s // 2
        if s % 2:
            blocks = [own[k][:answers, :]] + [o[k] for o in packs_odd]
        else:
            blocks = [o[k] for o in packs]
        out_buf[s] = dot(cot_buf[...], jnp.concatenate(blocks, axis=0), NN)
        out_copy(s).start()
    for s in range(size):
        out_copy(s).wait()


def pack_kernel(*refs):
    out_ref = refs[-1]
    for k in range(out_ref.shape[0]):
        out_ref[k] = refs[k][: out_ref.shape[1], :]


def cost(products, exps, nbytes):
    return pl.CostEstimate(flops=2 * products, transcendentals=exps, bytes_accessed=nbytes)


def shaped(shape, dtype):
    return jax.ShapeDtypeStruct(shape, dtype)


def fast_device(dp, size, queries, keys, values, lengths, out_weight, out_cotangent):
    bf16, f32 = jnp.bfloat16, jnp.float32
    passages, passage_len, inner = keys.shape[1:]
    key_count = passages * passage_len
    answers, width = queries.shape[1:]
    half = size // 2
    heads = width // HEAD_SIZE
    model = out_weight.shape[0]
    me = lax.axis_index("psg").reshape(1)
    query = queries[0]
    cot = out_cotangent[0]
    key_rows = keys.reshape(key_count, inner)
    value_rows = values.reshape(key_count, inner)

    def interleaved(even, odd):
        return [r for pair in zip(even, odd) for r in pair]

    q_even = spread(query, size)
    slots = interleaved(q_even, across(q_even, size))

    g_even, g_odd = call(
        functools.partial(grad_partial_kernel, size),
        me,
        cot,
        out_weight,
        out=[shaped((half, answers, width), bf16)] * 2,
        ins=[SMEM, HBM, HBM],
        outs=[VMEM] * 2,
        scratch=[
            pltpu.VMEM((answers, model), bf16),
            pltpu.VMEM((size, model, width), bf16),
            pltpu.SemaphoreType.DMA((size,)),
            pltpu.SemaphoreType.DMA(()),
        ],
        vmem=GRAD_VMEM,
        cost=cost(answers * model * inner, 0, 2 * model * inner),
    )
    g_other = swap(g_odd, "psg", size, 1)
    block = shaped((answers, width), bf16)
    g_sums = call(
        add_pair_kernel,
        g_even,
        g_other,
        out=[block] * half,
        ins=[VMEM] * 2,
        outs=[VMEM] * half,
        cost=cost(ADD_COST * answers * model * inner, 0, 2 * model * inner),
    )
    g_parts = [swap(g_sums[d // 2], "psg", size, d) for d in far_first(size)]

    packed = shaped((width + EXTRA, answers), bf16)
    pairs = width // PAIR

    def forward(parity):
        return call(
            functools.partial(forward_kernel, parity, passages),
            me,
            lengths,
            *slots[parity::2],
            key_rows,
            value_rows,
            out=[
                shaped((half, width + EXTRA, answers), bf16),
                shaped((half * pairs, key_count, 2 * answers), bf16),
                shaped((half, heads, answers), f32),
            ],
            ins=[SMEM, SMEM] + [VMEM] * (half + 2),
            outs=[VMEM] * 3,
            scratch=[
                pltpu.VMEM((half, answers, width), bf16),
                pltpu.VMEM((pairs, key_count, 2 * answers), f32),
                pltpu.VMEM((key_count, PAIR), f32),
            ],
            vmem=12,
            cost=cost(2 * answers * key_count * inner // 2, answers * key_count * half * heads, 2 * key_count * inner),
        )

    o_odd, *kept_odd = forward(1)
    o_even, *kept_even = forward(0)

    o_other = swap(o_odd, "psg", size, 1)
    o_pairs = call(merge_pair_kernel, o_even, o_other, out=[packed] * half, ins=[VMEM] * 2, outs=[VMEM] * half)
    arrived = [swap(o_pairs[d // 2], "psg", size, d) for d in far_first(size)]
    context_grad = call(add_all_kernel, g_sums[0], *g_parts, out=block, ins=[VMEM] * half, outs=VMEM)
    cg_even = spread(context_grad, size)
    context = call(
        functools.partial(merge_final_kernel, half),
        o_pairs[0],
        *arrived,
        context_grad,
        out=shaped((answers + 4 * heads, width), bf16),
        ins=[VMEM] * (half + 1),
        outs=VMEM,
    )
    c_even = spread(context, size)
    c_odd = across(c_even, size)
    c_slots = interleaved(c_even, c_odd)
    g_slots = interleaved(cg_even, across(cg_even, size))

    def backward(chosen, carried):
        count = len(chosen)
        pick = slice(chosen[0], chosen[0] + count)
        fixed = 1 + 3 * count + 6
        return call(
            functools.partial(backward_kernel, chosen, len(carried)),
            me,
            *slots[pick],
            *g_slots[pick],
            *c_slots[pick],
            key_rows,
            value_rows,
            kept_even[0],
            kept_odd[0],
            kept_even[1],
            kept_odd[1],
            *carried,
            out=[shaped((key_count, inner), bf16)] * 2 + [shaped((count // 2, width, answers), bf16)] * 2,
            ins=[SMEM] + [VMEM] * (3 * count + 6) + [ANY] * len(carried),
            outs=[ANY, ANY, VMEM, VMEM],
            scratch=[
                pltpu.VMEM((count, answers, width), bf16),
                pltpu.VMEM((count, answers, width), bf16),
                pltpu.VMEM((count, 2 * heads, answers), f32),
            ]
            + [pltpu.VMEM((pairs, key_count, 2 * answers), f32)]
            + [pltpu.VMEM((count, key_count, width), bf16)] * 2
            + [pltpu.SemaphoreType.DMA((2, count))],
            vmem=16,
            alias={fixed + i: i for i in range(len(carried))},
            cost=cost(4 * answers * key_count * count * width, 0, 8 * key_count * count * width),
        )

    def owners_sums(even, odd, count):
        other = swap(odd, "psg", size, 1)
        return call(
            add_pair_kernel,
            even,
            other,
            out=[shaped((width, answers), bf16)] * count,
            ins=[VMEM] * 2,
            outs=[VMEM] * count,
        )

    key_grad, value_grad, far_even, far_odd = backward(range(half, size), ())
    far_sums = owners_sums(far_even, far_odd, half // 2)
    key_grad, value_grad, near_even, near_odd = backward(range(half), (key_grad, value_grad))
    near_sums = owners_sums(near_even, near_odd, half // 2)
    sums = near_sums + far_sums
    dq_parts = [swap(sums[d // 2], "psg", size, d) for d in far_first(size)]
    query_grad = call(add_all_transposed_kernel, sums[0], *dq_parts, out=block, ins=[VMEM] * half, outs=VMEM)

    pack = call(pack_kernel, *c_even, out=shaped((half, answers, width), bf16), ins=[VMEM] * half, outs=VMEM)
    cots = [cot] + [swap(cot, "dp", dp, d) for d in range(1, dp)]
    packs = [pack] + [swap(pack, "dp", dp, d) for d in range(1, dp)]
    packs_odd = [swap(packs[d], "psg", size, 1) for d in range(1, dp)]
    layer_out = call(
        functools.partial(layer_out_kernel, size),
        me,
        *c_slots,
        out_weight,
        out=shaped((answers, model), bf16),
        ins=[SMEM] + [VMEM] * (size + 1),
        outs=VMEM,
    )
    weight_grad = call(
        functools.partial(weight_grad_kernel, size, dp, answers),
        me,
        *cots,
        *packs,
        *packs_odd,
        *c_odd,
        out=shaped((model, inner), f32),
        ins=[SMEM] + [VMEM] * (3 * dp - 1 + half),
        outs=ANY,
        scratch=[
            pltpu.VMEM((model, dp * answers), bf16),
            pltpu.VMEM((size, model, width), f32),
            pltpu.SemaphoreType.DMA((size,)),
        ],
        vmem=16,
    )
    return (
        layer_out[None],
        weight_grad,
        query_grad[None],
        key_grad.reshape(keys.shape),
        value_grad.reshape(values.shape),
    )


def spread_heads(factor):
    return jnp.transpose(factor, (0, 2, 1))[..., None]


def general_device(queries, keys, values, lengths, out_weight, out_cotangent):
    question_count, passages, passage_len, inner_dim = keys.shape
    key_count = passages * passage_len
    answer_len = queries.shape[1]
    head_split = (question_count, answer_len, inner_dim // HEAD_SIZE, HEAD_SIZE)
    key_split = (question_count, key_count, inner_dim // HEAD_SIZE, HEAD_SIZE)
    einsum = functools.partial(jnp.einsum, preferred_element_type=jnp.float32)
    query_heads = lax.all_gather(queries, "psg", axis=2, tiled=True).reshape(head_split)
    key_heads = keys.reshape(key_split)
    value_heads = values.reshape(key_split)
    positions = jnp.arange(passage_len, dtype=jnp.int32)
    valid = (positions[None, None, :] < lengths[:, :, None]).reshape(question_count, 1, 1, key_count)
    scores = einsum("bihe,bkhe->bhik", query_heads, key_heads)
    row_max = lax.pmax(jnp.max(jnp.where(valid, scores, -jnp.inf), axis=3), "psg")
    weights = jnp.where(valid, jnp.exp(scores - row_max[..., None]), 0.0)
    output = einsum("bhik,bkhe->bihe", weights.astype(jnp.bfloat16), value_heads)
    row_sum, output = lax.psum((jnp.sum(weights, axis=3), output), "psg")
    context = (output / spread_heads(row_sum)).astype(jnp.bfloat16)
    context_rows = context.reshape(question_count * answer_len, inner_dim)
    grad_rows = out_cotangent.reshape(question_count * answer_len, -1)
    layer_out = jnp.dot(context_rows, out_weight.T, preferred_element_type=jnp.float32).astype(jnp.bfloat16)
    weight_grad = lax.psum(
        jnp.dot(grad_rows.T, context_rows, preferred_element_type=jnp.float32).astype(jnp.bfloat16), "dp"
    ).astype(jnp.float32)
    context_grad = lax.psum(jnp.dot(grad_rows, out_weight, preferred_element_type=jnp.float32), "psg").astype(
        jnp.bfloat16
    )
    grad_heads = context_grad.reshape(head_split)
    products = grad_heads.astype(jnp.float32) * context.astype(jnp.float32)
    row_dots = jnp.transpose(jnp.sum(products, axis=3), (0, 2, 1))
    probs = weights / row_sum[..., None]
    prob_grad = einsum("bihe,bkhe->bhik", grad_heads, value_heads)
    score_grad = (probs * (prob_grad - row_dots[..., None])).astype(jnp.bfloat16)
    value_grad = einsum("bhik,bihe->bkhe", probs.astype(jnp.bfloat16), grad_heads)
    key_grad = einsum("bhik,bihe->bkhe", score_grad, query_heads)
    query_terms = einsum("bhik,bkhe->bihe", score_grad, key_heads).reshape(question_count, answer_len, inner_dim)
    query_grad = lax.psum_scatter(query_terms, "psg", scatter_dimension=2, tiled=True)
    return (
        layer_out.reshape(question_count, answer_len, -1),
        weight_grad,
        query_grad.astype(jnp.bfloat16),
        key_grad.astype(jnp.bfloat16).reshape(keys.shape),
        value_grad.astype(jnp.bfloat16).reshape(values.shape),
    )


def solution(mesh):
    dp, size = mesh.shape["dp"], mesh.shape["psg"]

    def per_device(queries, keys, values, lengths, out_weight, out_cotangent):
        return fast_device(dp, size, queries, keys, values, lengths, out_weight, out_cotangent)

    def step(queries, keys, values, lengths, out_weight, out_cotangent):
        width = queries.shape[2] // size
        direct = (
            size in (4, 8)
            and dp in (2, 4)
            and keys.shape[0] == dp
            and width % PAIR == 0
            and 3 * (width // HEAD_SIZE) <= EXTRA
            and 2 * (width // HEAD_SIZE) % 8 == 0
            and queries.shape[1] % 128 == 0
            and keys.shape[2] % 16 == 0
            and (out_weight.shape[0] // size) % width == 0
        )
        body = jax.shard_map(
            per_device if direct else general_device,
            mesh=mesh,
            in_specs=(
                P("dp", None, "psg"),
                P("dp", "psg", None, None),
                P("dp", "psg", None, None),
                P("dp", "psg"),
                P("psg", None),
                P("dp", None, "psg"),
            ),
            out_specs=(
                P("dp", None, "psg"),
                P("psg", None),
                P("dp", None, "psg"),
                P("dp", "psg", None, None),
                P("dp", "psg", None, None),
            ),
            check_vma=False,
        )
        return body(queries, keys, values, lengths, out_weight, out_cotangent)

    return step
```

```python
import functools

import jax
import jax.numpy as jnp
from jax import lax
from jax.experimental import pallas as pl
from jax.experimental.pallas import tpu as pltpu
from jax.sharding import PartitionSpec as P

HEAD_SIZE = 64
PAIR = 2 * HEAD_SIZE
MASKED = -1e30
EXTRA = 16
MIB = 1 << 20
GRAD_VMEM = 49

NT = (((1,), (1,)), ((), ()))
NN = (((1,), (0,)), ((), ()))
TN = (((0,), (0,)), ((), ()))
ANY = pl.BlockSpec(memory_space=pl.ANY)
VMEM = pl.BlockSpec(memory_space=pltpu.VMEM)
SMEM = pl.BlockSpec(memory_space=pltpu.SMEM)
HBM = pl.BlockSpec(memory_space=pltpu.HBM)


def dot(a, b, dims):
    return lax.dot_general(a, b, dims, preferred_element_type=jnp.float32)


def swap(x, axis, size, distance):
    return lax.ppermute(x, axis, [(j, j ^ distance) for j in range(size)])


def call(kernel, *args, out, ins, outs, scratch=(), vmem=8, alias=None, cost=None):
    return pl.pallas_call(
        kernel,
        out_shape=out,
        in_specs=ins,
        out_specs=outs,
        scratch_shapes=list(scratch),
        input_output_aliases=alias or {},
        compiler_params=pltpu.CompilerParams(vmem_limit_bytes=int(vmem * MIB)),
        cost_estimate=cost,
    )(*args)


def far_first(size):
    return range(size - 2, 0, -2)


def spread(x, size):
    even = [x] + [None] * (size // 2 - 1)
    for d in far_first(size):
        even[d // 2] = swap(x, "psg", size, d)
    return even


def across(blocks, size):
    return [swap(b, "psg", size, 1) for b in blocks]


def block_stack(x, lane_low):
    zero = jnp.zeros_like(x)
    return jnp.concatenate([jnp.where(lane_low, x, zero), jnp.where(lane_low, zero, x)], axis=0)


def diagonal(x):
    rows = x.shape[1] // 2
    return jnp.concatenate([x[:HEAD_SIZE, :rows], x[HEAD_SIZE:, rows:]], axis=0)


def mask_bias(lengths_ref, passages, passage_len):
    row = lax.broadcasted_iota(jnp.int32, (passage_len, PAIR), 0)
    return jnp.concatenate([jnp.where(row < lengths_ref[0, p], 0.0, MASKED) for p in range(passages)], axis=0)


def split3(x):
    high = x.astype(jnp.bfloat16).astype(jnp.float32)
    middle = (x - high).astype(jnp.bfloat16).astype(jnp.float32)
    return high, middle, (x - high - middle).astype(jnp.bfloat16).astype(jnp.float32)


def thirds(x):
    pad = jnp.zeros((EXTRA - 3 * x.shape[0], x.shape[1]), jnp.float32)
    return jnp.concatenate([*split3(x), pad], axis=0).astype(jnp.bfloat16)


def unite(rows, heads):
    wide = rows.astype(jnp.float32)
    return wide[:heads] + wide[heads : 2 * heads] + wide[2 * heads : 3 * heads]


def columns_of(ref, me, slot, width):
    owner = jnp.bitwise_xor(me, slot)
    return ref.at[:, pl.ds(pl.multiple_of(owner * width, width), width)]


def forward_kernel(parity, passages, lengths_ref, *refs):
    out_ref, weights_ref, tops_ref, q_buf, s_buf, bias_ref = refs[-6:]
    keys_ref, values_ref = refs[-8:-6]
    count, _, width = q_buf.shape
    pairs = width // PAIR
    for k in range(count):
        q_buf[k] = refs[k][...]
    bias_ref[...] = mask_bias(lengths_ref, passages, keys_ref.shape[1] // passages)
    lane_low = lax.broadcasted_iota(jnp.int32, (1, PAIR), 1) < HEAD_SIZE

    def score(k, p):
        queries = block_stack(q_buf[k, :, p * PAIR : (p + 1) * PAIR], lane_low)
        bias = bias_ref[...]
        keys = keys_ref[2 * k + parity, :, p * PAIR : (p + 1) * PAIR]
        scores = dot(keys, queries, NT) + jnp.concatenate([bias, bias], axis=1)
        s_buf[p] = scores
        return jnp.max(scores, axis=0, keepdims=True)

    def mix(k, p, top):
        weights = jnp.exp(s_buf[p] - top)
        total = jnp.sum(weights, axis=0, keepdims=True)
        rounded = weights.astype(jnp.bfloat16)
        weights_ref[k * pairs + p] = rounded
        values = values_ref[2 * k + parity, :, p * PAIR : (p + 1) * PAIR]
        mixed = dot(values, rounded, TN) / total
        out_ref[k, p * PAIR : (p + 1) * PAIR, :] = diagonal(mixed).astype(jnp.bfloat16)
        return top + jnp.log(total)

    def by_head(rows):
        n = rows[0].shape[1] // 2
        return jnp.concatenate([x[:, h * n : (h + 1) * n] for x in rows for h in range(2)], axis=0)

    def one_slot(k, top):
        tops, lses = [top], []
        for p in range(pairs):
            if p + 1 < pairs:
                tops.append(score(k, p + 1))
            elif pairs > 1:
                top = score(jnp.minimum(k + 1, count - 1), 0)
            lses.append(mix(k, p, tops[p]))
        if pairs == 1:
            top = score(jnp.minimum(k + 1, count - 1), 0)
        tops_ref[k] = by_head(tops)
        out_ref[k, width:, :] = thirds(by_head(lses))
        return top

    lax.fori_loop(0, count // 2, lambda k, top: one_slot(2 * k + 1, one_slot(2 * k, top)), score(0, 0))


def merge(blocks):
    width = blocks[0].shape[0] - EXTRA
    heads = width // HEAD_SIZE
    lses = [unite(b[width:], heads) for b in blocks]
    top = functools.reduce(jnp.maximum, lses)
    shares = [jnp.exp(x - top) for x in lses]
    total = sum(shares)
    shares = [x / total for x in shares]
    outs = []
    for h in range(heads):
        rows = slice(h * HEAD_SIZE, (h + 1) * HEAD_SIZE)
        outs.append(sum(x[h : h + 1] * b[rows].astype(jnp.float32) for b, x in zip(blocks, shares)))
    return jnp.concatenate(outs, axis=0), top + jnp.log(total)


def merge_pair_kernel(a_ref, b_ref, *out_refs):
    for k, out_ref in enumerate(out_refs):
        out, lse = merge([a_ref[k], b_ref[k]])
        width = out.shape[0]
        out_ref[:width, :] = out.astype(jnp.bfloat16)
        out_ref[width:, :] = thirds(lse)


def merge_final_kernel(count, *refs):
    grad_ref, out_ref = refs[count:]
    out, lse = merge([r[...] for r in refs[:count]])
    context = out.T.astype(jnp.bfloat16)
    answers, _ = context.shape
    out_ref[:answers, :] = context
    product = (context.astype(jnp.float32) * grad_ref[...].astype(jnp.float32)).T
    dots = [
        jnp.sum(product[h * HEAD_SIZE : (h + 1) * HEAD_SIZE], axis=0, keepdims=True) for h in range(lse.shape[0])
    ]
    high, middle, low = split3(jnp.concatenate([lse] + dots, axis=0))
    top = jnp.concatenate([high, middle], axis=1)
    bottom = jnp.concatenate([low, jnp.zeros_like(low)], axis=1)
    out_ref[answers:, :] = jnp.concatenate([top, bottom], axis=0).astype(jnp.bfloat16)


def stats_of(block_ref, answers):
    rows = block_ref[answers:, :].astype(jnp.float32)
    n = rows.shape[0] // 2
    return rows[:n, :answers] + rows[:n, answers:] + rows[n:, :answers]


def backward_kernel(slots, carried, me_ref, *refs):
    count = len(slots)
    q_refs, g_refs, c_refs = refs[:count], refs[count : 2 * count], refs[2 * count : 3 * count]
    keys_ref, values_ref, *kept = refs[3 * count : 3 * count + 6]
    weights_refs, tops_refs = kept[:2], kept[2:]
    dk_ref, dv_ref, even_ref, odd_ref, q_buf, g_buf, st_buf, p_buf, dk_buf, dv_buf, sem = refs[3 * count + 6 + carried :]
    me = me_ref[0]
    answers, width = q_buf.shape[1:]
    pairs = width // PAIR
    first = slots[0]
    heads = width // HEAD_SIZE

    def dk_copy(i):
        return pltpu.make_async_copy(dk_buf.at[i], columns_of(dk_ref, me, first + i, width), sem.at[0, i])

    def dv_copy(i):
        return pltpu.make_async_copy(dv_buf.at[i], columns_of(dv_ref, me, first + i, width), sem.at[1, i])

    lane_low = lax.broadcasted_iota(jnp.int32, (1, PAIR), 1) < HEAD_SIZE
    for i in range(count):
        stats = stats_of(c_refs[i], answers)
        share = jnp.exp(tops_refs[i % 2][first // 2 + i // 2] - stats[:heads])
        st_buf[i] = jnp.concatenate([share, stats[heads:]], axis=0)
        q_buf[i] = q_refs[i][...]
        g_buf[i] = g_refs[i][...]

    def grads_of(i, p):
        return block_stack(g_buf[i, :, p * PAIR : (p + 1) * PAIR], lane_low)

    def prob_grad(i, p):
        p_buf[p] = dot(values_ref[first + i, :, p * PAIR : (p + 1) * PAIR], grads_of(i, p), NT)

    def row_pair(rows, at):
        return jnp.concatenate([rows[at : at + 1], rows[at + 1 : at + 2]], axis=1)

    def rest(i, p, parity, k):
        out_ref = (even_ref, odd_ref)[parity]
        lanes = slice(p * PAIR, (p + 1) * PAIR)
        queries = block_stack(q_buf[i, :, lanes], lane_low)
        stats = st_buf[i]
        probs = weights_refs[parity][(first // 2 + k) * pairs + p].astype(jnp.float32) * row_pair(stats, 2 * p)
        score_grad = (probs * (p_buf[p] - row_pair(stats, heads + 2 * p))).astype(jnp.bfloat16)
        dv_buf[i, :, lanes] = dot(probs.astype(jnp.bfloat16), grads_of(i, p), NN).astype(jnp.bfloat16)
        dk_buf[i, :, lanes] = dot(score_grad, queries, NN).astype(jnp.bfloat16)
        out_ref[k, lanes, :] = diagonal(dot(keys_ref[first + i, :, lanes], score_grad, TN)).astype(
            jnp.bfloat16
        )

    def one_slot(i, parity, k):
        for p in range(pairs):
            if p + 1 < pairs:
                prob_grad(i, p + 1)
                rest(i, p, parity, k)
            else:
                rest(i, p, parity, k) if pairs == 1 else None
                prob_grad(jnp.minimum(i + 1, count - 1), 0)
                rest(i, p, parity, k) if pairs > 1 else None
        dk_copy(i).start()
        dv_copy(i).start()

    def body(k, carry):
        one_slot(2 * k, 0, k)
        one_slot(2 * k + 1, 1, k)
        return carry

    prob_grad(0, 0)
    lax.fori_loop(0, count // 2, body, 0)
    for i in range(count):
        dk_copy(i).wait()
        dv_copy(i).wait()


def add_pair_kernel(a_ref, b_ref, *out_refs):
    for k, out_ref in enumerate(out_refs):
        out_ref[...] = (a_ref[k].astype(jnp.float32) + b_ref[k].astype(jnp.float32)).astype(jnp.bfloat16)


def add_all_kernel(*refs):
    total = refs[0][...].astype(jnp.float32)
    for r in refs[1:-1]:
        total += r[...].astype(jnp.float32)
    refs[-1][...] = total.astype(jnp.bfloat16)


def add_all_transposed_kernel(*refs):
    total = refs[0][...].astype(jnp.float32)
    for r in refs[1:-1]:
        total += r[...].astype(jnp.float32)
    refs[-1][...] = total.T.astype(jnp.bfloat16)


def grad_partial_kernel(size, me_ref, cot_ref, weight_ref, keys_ref, values_ref, *refs):
    even_ref, odd_ref, k_out, v_out, cot_buf, w_buf, sem, cot_sem = refs
    me = me_ref[0]
    width = w_buf.shape[2]

    def copy(ref, buf, lane, s):
        return pltpu.make_async_copy(columns_of(ref, me, s, width), buf.at[s], sem.at[lane, s])

    order = list(range(1, size, 2)) + list(range(0, size, 2))
    cot_copy = pltpu.make_async_copy(cot_ref, cot_buf, cot_sem)
    cot_copy.start()
    for s in order:
        copy(weight_ref, w_buf, 0, s).start()
    for s in range(size):
        copy(keys_ref, k_out, 1, s).start()
        copy(values_ref, v_out, 2, s).start()
    cot_copy.wait()
    cot = cot_buf[...]
    for s in order:
        copy(weight_ref, w_buf, 0, s).wait()
        (odd_ref if s % 2 else even_ref)[s // 2] = dot(cot, w_buf[s], NN).astype(jnp.bfloat16)
    for s in range(size):
        copy(keys_ref, k_out, 1, s).wait()
        copy(values_ref, v_out, 2, s).wait()


def layer_out_kernel(size, me_ref, *refs):
    weight_ref, out_ref = refs[size:]
    me = me_ref[0]
    answers, width = out_ref.shape[0], refs[0].shape[1]
    total = None
    for s in range(size):
        part = dot(refs[s][:answers, :], columns_of(weight_ref, me, s, width)[...], NT)
        total = part if total is None else total + part
    out_ref[...] = total.astype(jnp.bfloat16)


def weight_grad_kernel(size, groups, answers, me_ref, *refs):
    half = size // 2
    cots, refs = refs[:groups], refs[groups:]
    packs, packs_odd, own = refs[:groups], refs[groups : 2 * groups - 1], refs[2 * groups - 1 : 2 * groups - 1 + half]
    out_ref, cot_buf, out_buf, sem = refs[2 * groups - 1 + half :]
    me = me_ref[0]
    width = out_buf.shape[2]
    for g in range(groups):
        cot_buf[:, g * answers : (g + 1) * answers] = cots[g][...].T

    def out_copy(s):
        return pltpu.make_async_copy(out_buf.at[s], columns_of(out_ref, me, s, width), sem.at[s])

    for s in range(size):
        k = s // 2
        if s % 2:
            blocks = [own[k][:answers, :]] + [o[k] for o in packs_odd]
        else:
            blocks = [o[k] for o in packs]
        out_buf[s] = dot(cot_buf[...], jnp.concatenate(blocks, axis=0), NN)
        out_copy(s).start()
    for s in range(size):
        out_copy(s).wait()


def pack_kernel(*refs):
    out_ref = refs[-1]
    for k in range(out_ref.shape[0]):
        out_ref[k] = refs[k][: out_ref.shape[1], :]


def cost(products, exps, nbytes):
    return pl.CostEstimate(flops=2 * products, transcendentals=exps, bytes_accessed=nbytes)


def shaped(shape, dtype):
    return jax.ShapeDtypeStruct(shape, dtype)


def fast_device(dp, size, queries, keys, values, lengths, out_weight, out_cotangent):
    bf16, f32 = jnp.bfloat16, jnp.float32
    passages, passage_len, inner = keys.shape[1:]
    key_count = passages * passage_len
    answers, width = queries.shape[1:]
    half = size // 2
    heads = width // HEAD_SIZE
    model = out_weight.shape[0]
    me = lax.axis_index("psg").reshape(1)
    query = queries[0]
    cot = out_cotangent[0]
    key_rows = keys.reshape(key_count, inner)
    value_rows = values.reshape(key_count, inner)

    def interleaved(even, odd):
        return [r for pair in zip(even, odd) for r in pair]

    q_even = spread(query, size)
    slots = interleaved(q_even, across(q_even, size))

    resident = shaped((size, key_count, width), bf16)
    g_even, g_odd, slot_keys, slot_values = call(
        functools.partial(grad_partial_kernel, size),
        me,
        cot,
        out_weight,
        key_rows,
        value_rows,
        out=[shaped((half, answers, width), bf16)] * 2 + [resident] * 2,
        ins=[SMEM] + [HBM] * 4,
        outs=[VMEM] * 4,
        scratch=[
            pltpu.VMEM((answers, model), bf16),
            pltpu.VMEM((size, model, width), bf16),
            pltpu.SemaphoreType.DMA((3, size)),
            pltpu.SemaphoreType.DMA(()),
        ],
        vmem=GRAD_VMEM,
    )
    g_other = swap(g_odd, "psg", size, 1)
    block = shaped((answers, width), bf16)
    g_sums = call(add_pair_kernel, g_even, g_other, out=[block] * half, ins=[VMEM] * 2, outs=[VMEM] * half)
    g_parts = [swap(g_sums[d // 2], "psg", size, d) for d in far_first(size)]

    packed = shaped((width + EXTRA, answers), bf16)
    pairs = width // PAIR

    def forward(parity):
        return call(
            functools.partial(forward_kernel, parity, passages),
            lengths,
            *slots[parity::2],
            slot_keys,
            slot_values,
            out=[
                shaped((half, width + EXTRA, answers), bf16),
                shaped((half * pairs, key_count, 2 * answers), bf16),
                shaped((half, heads, answers), f32),
            ],
            ins=[SMEM] + [VMEM] * (half + 2),
            outs=[VMEM] * 3,
            scratch=[
                pltpu.VMEM((half, answers, width), bf16),
                pltpu.VMEM((pairs, key_count, 2 * answers), f32),
                pltpu.VMEM((key_count, PAIR), f32),
            ],
            vmem=12,
            cost=cost(2 * answers * key_count * inner // 2, answers * key_count * half * heads, 2 * key_count * inner),
        )

    o_odd, *kept_odd = forward(1)
    o_even, *kept_even = forward(0)

    o_other = swap(o_odd, "psg", size, 1)
    o_pairs = call(merge_pair_kernel, o_even, o_other, out=[packed] * half, ins=[VMEM] * 2, outs=[VMEM] * half)
    arrived = [swap(o_pairs[d // 2], "psg", size, d) for d in far_first(size)]
    context_grad = call(add_all_kernel, g_sums[0], *g_parts, out=block, ins=[VMEM] * half, outs=VMEM)
    cg_even = spread(context_grad, size)
    context = call(
        functools.partial(merge_final_kernel, half),
        o_pairs[0],
        *arrived,
        context_grad,
        out=shaped((answers + 4 * heads, width), bf16),
        ins=[VMEM] * (half + 1),
        outs=VMEM,
    )
    c_even = spread(context, size)
    c_odd = across(c_even, size)
    c_slots = interleaved(c_even, c_odd)
    g_slots = interleaved(cg_even, across(cg_even, size))

    def backward(chosen, carried):
        count = len(chosen)
        pick = slice(chosen[0], chosen[0] + count)
        fixed = 1 + 3 * count + 6
        return call(
            functools.partial(backward_kernel, chosen, len(carried)),
            me,
            *slots[pick],
            *g_slots[pick],
            *c_slots[pick],
            slot_keys,
            slot_values,
            kept_even[0],
            kept_odd[0],
            kept_even[1],
            kept_odd[1],
            *carried,
            out=[shaped((key_count, inner), bf16)] * 2 + [shaped((count // 2, width, answers), bf16)] * 2,
            ins=[SMEM] + [VMEM] * (3 * count + 6) + [ANY] * len(carried),
            outs=[ANY, ANY, VMEM, VMEM],
            scratch=[
                pltpu.VMEM((count, answers, width), bf16),
                pltpu.VMEM((count, answers, width), bf16),
                pltpu.VMEM((count, 2 * heads, answers), f32),
            ]
            + [pltpu.VMEM((pairs, key_count, 2 * answers), f32)]
            + [pltpu.VMEM((count, key_count, width), bf16)] * 2
            + [pltpu.SemaphoreType.DMA((2, count))],
            vmem=16,
            alias={fixed + i: i for i in range(len(carried))},
            cost=cost(4 * answers * key_count * count * width, 0, 8 * key_count * count * width),
        )

    def owners_sums(even, odd, count):
        other = swap(odd, "psg", size, 1)
        return call(
            add_pair_kernel,
            even,
            other,
            out=[shaped((width, answers), bf16)] * count,
            ins=[VMEM] * 2,
            outs=[VMEM] * count,
        )

    key_grad, value_grad, far_even, far_odd = backward(range(half, size), ())
    far_sums = owners_sums(far_even, far_odd, half // 2)
    key_grad, value_grad, near_even, near_odd = backward(range(half), (key_grad, value_grad))
    near_sums = owners_sums(near_even, near_odd, half // 2)
    sums = near_sums + far_sums
    dq_parts = [swap(sums[d // 2], "psg", size, d) for d in far_first(size)]
    query_grad = call(add_all_transposed_kernel, sums[0], *dq_parts, out=block, ins=[VMEM] * half, outs=VMEM)

    pack = call(pack_kernel, *c_even, out=shaped((half, answers, width), bf16), ins=[VMEM] * half, outs=VMEM)
    cots = [cot] + [swap(cot, "dp", dp, d) for d in range(1, dp)]
    packs = [pack] + [swap(pack, "dp", dp, d) for d in range(1, dp)]
    packs_odd = [swap(packs[d], "psg", size, 1) for d in range(1, dp)]
    layer_out = call(
        functools.partial(layer_out_kernel, size),
        me,
        *c_slots,
        out_weight,
        out=shaped((answers, model), bf16),
        ins=[SMEM] + [VMEM] * (size + 1),
        outs=VMEM,
    )
    weight_grad = call(
        functools.partial(weight_grad_kernel, size, dp, answers),
        me,
        *cots,
        *packs,
        *packs_odd,
        *c_odd,
        out=shaped((model, inner), f32),
        ins=[SMEM] + [VMEM] * (3 * dp - 1 + half),
        outs=ANY,
        scratch=[
            pltpu.VMEM((model, dp * answers), bf16),
            pltpu.VMEM((size, model, width), f32),
            pltpu.SemaphoreType.DMA((size,)),
        ],
        vmem=16,
    )
    return (
        layer_out[None],
        weight_grad,
        query_grad[None],
        key_grad.reshape(keys.shape),
        value_grad.reshape(values.shape),
    )


def spread_heads(factor):
    return jnp.transpose(factor, (0, 2, 1))[..., None]


def general_device(queries, keys, values, lengths, out_weight, out_cotangent):
    question_count, passages, passage_len, inner_dim = keys.shape
    key_count = passages * passage_len
    answer_len = queries.shape[1]
    head_split = (question_count, answer_len, inner_dim // HEAD_SIZE, HEAD_SIZE)
    key_split = (question_count, key_count, inner_dim // HEAD_SIZE, HEAD_SIZE)
    einsum = functools.partial(jnp.einsum, preferred_element_type=jnp.float32)
    query_heads = lax.all_gather(queries, "psg", axis=2, tiled=True).reshape(head_split)
    key_heads = keys.reshape(key_split)
    value_heads = values.reshape(key_split)
    positions = jnp.arange(passage_len, dtype=jnp.int32)
    valid = (positions[None, None, :] < lengths[:, :, None]).reshape(question_count, 1, 1, key_count)
    scores = einsum("bihe,bkhe->bhik", query_heads, key_heads)
    row_max = lax.pmax(jnp.max(jnp.where(valid, scores, -jnp.inf), axis=3), "psg")
    weights = jnp.where(valid, jnp.exp(scores - row_max[..., None]), 0.0)
    output = einsum("bhik,bkhe->bihe", weights.astype(jnp.bfloat16), value_heads)
    row_sum, output = lax.psum((jnp.sum(weights, axis=3), output), "psg")
    context = (output / spread_heads(row_sum)).astype(jnp.bfloat16)
    context_rows = context.reshape(question_count * answer_len, inner_dim)
    grad_rows = out_cotangent.reshape(question_count * answer_len, -1)
    layer_out = jnp.dot(context_rows, out_weight.T, preferred_element_type=jnp.float32).astype(jnp.bfloat16)
    weight_grad = lax.psum(
        jnp.dot(grad_rows.T, context_rows, preferred_element_type=jnp.float32).astype(jnp.bfloat16), "dp"
    ).astype(jnp.float32)
    context_grad = lax.psum(jnp.dot(grad_rows, out_weight, preferred_element_type=jnp.float32), "psg").astype(
        jnp.bfloat16
    )
    grad_heads = context_grad.reshape(head_split)
    products = grad_heads.astype(jnp.float32) * context.astype(jnp.float32)
    row_dots = jnp.transpose(jnp.sum(products, axis=3), (0, 2, 1))
    probs = weights / row_sum[..., None]
    prob_grad = einsum("bihe,bkhe->bhik", grad_heads, value_heads)
    score_grad = (probs * (prob_grad - row_dots[..., None])).astype(jnp.bfloat16)
    value_grad = einsum("bhik,bihe->bkhe", probs.astype(jnp.bfloat16), grad_heads)
    key_grad = einsum("bhik,bihe->bkhe", score_grad, query_heads)
    query_terms = einsum("bhik,bkhe->bihe", score_grad, key_heads).reshape(question_count, answer_len, inner_dim)
    query_grad = lax.psum_scatter(query_terms, "psg", scatter_dimension=2, tiled=True)
    return (
        layer_out.reshape(question_count, answer_len, -1),
        weight_grad,
        query_grad.astype(jnp.bfloat16),
        key_grad.astype(jnp.bfloat16).reshape(keys.shape),
        value_grad.astype(jnp.bfloat16).reshape(values.shape),
    )


def solution(mesh):
    dp, size = mesh.shape["dp"], mesh.shape["psg"]

    def per_device(queries, keys, values, lengths, out_weight, out_cotangent):
        return fast_device(dp, size, queries, keys, values, lengths, out_weight, out_cotangent)

    def step(queries, keys, values, lengths, out_weight, out_cotangent):
        width = queries.shape[2] // size
        direct = (
            size in (4, 8)
            and dp in (2, 4)
            and keys.shape[0] == dp
            and width % PAIR == 0
            and 3 * (width // HEAD_SIZE) <= EXTRA
            and 2 * (width // HEAD_SIZE) % 8 == 0
            and queries.shape[1] % 128 == 0
            and keys.shape[2] % 16 == 0
            and (out_weight.shape[0] // size) % width == 0
        )
        body = jax.shard_map(
            per_device if direct else general_device,
            mesh=mesh,
            in_specs=(
                P("dp", None, "psg"),
                P("dp", "psg", None, None),
                P("dp", "psg", None, None),
                P("dp", "psg"),
                P("psg", None),
                P("dp", None, "psg"),
            ),
            out_specs=(
                P("dp", None, "psg"),
                P("psg", None),
                P("dp", None, "psg"),
                P("dp", "psg", None, None),
                P("dp", "psg", None, None),
            ),
            check_vma=False,
        )
        return body(queries, keys, values, lengths, out_weight, out_cotangent)

    return step
```
